128 devices in a mesh: group: 8 (over z, core), member: 16 (over x, y).
Axes of the slice: x: 4, y: 4, z: 4, core: 2. Of those that a mesh axis runs over, the one named last changes fastest.
Arguments:
- hidden: bfloat16 [12288, 2048], P('group'), may hold values from -6 to 6
- token_slab: int32 [12288, 1], P(('group', 'member')), may hold values from 0 to 127; in each aligned block of 96 rows (0 to 95, 96 to 191, ...) at most 2 rows name the same one
- token_row: int32 [12288], P(('group', 'member')), may hold values from 0 to 2047
- slab_owner: int32 [128], replicated, may hold values from 0 to 127, each once
- ple_table: bfloat16 [262144, 256], P(('group', 'member')), may hold values from -0.375 to 0.375
- norm_gains: float32 [1, 3, 2048], replicated, may hold values from 0.1 to 1.9
- w_gate: bfloat16 [1, 2048, 8192], P(None, None, 'member'), may hold values from -0.125 to 0.125
- w_up: bfloat16 [1, 2048, 8192], P(None, None, 'member'), may hold values from -0.125 to 0.125
- w_down: bfloat16 [1, 8192, 2048], P(None, 'member'), may hold values from -0.0625 to 0.0625
- ple_gate: bfloat16 [1, 2048, 256], P(None, None, 'member'), may hold values from -0.125 to 0.125
- ple_proj: bfloat16 [1, 256, 2048], P(None, 'member'), may hold values from -0.375 to 0.375
Outputs:
- hidden_out: bfloat16 [12288, 2048], P('group')
The draws below stay inside these ranges and needn't reach their ends.
Inputs may be any that keep to these rules, and one draw needn't show every extreme that they name: Within the 96 tokens of one device (aligned blocks of token_slab), no slab is named by more than 2 tokens. Each number appears once: slab s is stored in rows slab_owner[s] * 2048 to slab_owner[s] * 2048 + 2047 of ple_table.
All inputs are finite; a program needn't handle non-finite values.
Results may differ from the reference program's by a relative error of at most 0.0061.
Values may be sent and summed in bfloat16 or wider, within the bound.
A program may use at most 128 MiB of HBM per device.

```python
import math
import jax
import jax.numpy as jnp
import numpy as np
from jax import lax

D = 2048
FF = 8192
PLE = 256
VOCAB = 262144
LAYERS = 1
SEQS = 12288
TOK_DEV = 96
CAP = 2
SLAB = 2048
PLEW = 256
DEVICES = 128


def plant(array, stream_key, low, top_value):
    longest = array.shape.index(max(array.shape))
    spots = []
    for shift in (0, 1):
        where = [jax.random.randint(jax.random.fold_in(stream_key, axis), (), 0, length) for axis, length in enumerate(array.shape)]
        where[longest] = (where[longest] + shift) % array.shape[longest]
        spots.append(tuple(where))
    return array.at[spots[0]].set(low).at[spots[1]].set(top_value)


def steps_of(rng, shape, cuts, smallest, top_value):
    def one(position, shards_of):
        draws = jax.random.uniform(jax.random.fold_in(jax.random.fold_in(rng, 6), position), (shards_of,), jnp.float32, smallest / len(cuts), top_value / len(cuts))
        return jnp.repeat(jnp.exp(draws), shape[position] // shards_of).reshape((-1,) + (1,) * (len(shape) - position - 1))

    factor_of = one(*cuts[0])
    for cut in cuts[1:]:
        factor_of = factor_of * one(*cut)
    return factor_of


def rank_table(amount, slope):
    loads = [(1 << 20) // math.isqrt(rank ** slope) + 1 for rank in range(1, amount + 1)]
    deviation = 1 + sum(loads) // (1 << 30)
    return np.cumsum(np.array([max(1, weight // deviation) for weight in loads]))


def ranked_ids(rng, extent, amount, lean):
    grid = rank_table(amount, lean)
    ticket = jax.random.randint(jax.random.fold_in(rng, 1), extent, 0, int(grid[amount - 1]))
    rank = jnp.searchsorted(jnp.asarray(grid, jnp.int32), ticket, side="right")
    return jax.random.permutation(jax.random.fold_in(rng, 2), amount)[rank].astype(jnp.int32)


def deal_out(stream_key, own, number, rows, number_of, top, bound, slope):
    ranking = jax.random.permutation(stream_key, number_of)
    crowded, usual = shares(number_of, rows * top, bound, slope, True), shares(number_of, rows * top, bound, slope, False)
    places = jnp.arange(number_of)

    def named(tallies, rotation):
        used = int((tallies > 0).sum())
        fixed = max(1, used // 4)
        passed = fixed + (places - fixed + rotation * (used - fixed)) % max(1, number_of - fixed)
        return jnp.zeros((number_of,), jnp.int32).at[ranking[jnp.where(places < fixed, places, passed)]].set(jnp.asarray(tallies, jnp.int32))

    tallies = jnp.where(number % 4 == 0, named(crowded, number // 4), named(usual, number - number // 4 - 1))
    mixed = jax.random.permutation(jax.random.fold_in(own, 3), number_of)
    donor, receiver = mixed[0:number_of // 2 * 2:2], mixed[1:number_of // 2 * 2:2]
    room = jnp.minimum(tallies[donor] - 1, bound - tallies[receiver]) // 2
    room = jnp.where((donor == ranking[0]) | (receiver == ranking[0]) | (tallies[receiver] == 0), 0, jnp.maximum(room, 0))
    passed = jax.random.randint(jax.random.fold_in(own, 4), (number_of // 2,), 0, 1 << 20) % (room + 1)
    tallies = tallies.at[donor].add(-passed).at[receiver].add(passed)
    labels = jnp.searchsorted(jnp.cumsum(tallies), jnp.arange(rows * top), side="right").astype(jnp.int32)
    table = labels.reshape(top, rows).T
    table = table[jax.random.permutation(jax.random.fold_in(own, 1), rows)]
    rotation = jax.random.randint(jax.random.fold_in(own, 2), (rows, 1), 0, top)
    return jnp.take_along_axis(table, (jnp.arange(top)[None, :] + rotation) % top, axis=1)


def shares(count, total, limit, slope, full):
    loads = [(1 << 20) // math.isqrt(rank ** slope) + 1 for rank in range(1, count + 1)]
    largest = limit if full else min(limit, max(-(-total // count), total * loads[0] // sum(loads)))
    least = 1 if total - largest >= count - 1 else 0
    given, spare = [largest] + [least] * (count - 1), total - largest - least * (count - 1)
    while spare > 0:
        free = [i for i in range(1, count) if given[i] < largest] or [i for i in range(1, count) if given[i] < limit]
        mass, budget = sum([loads[i] for i in free]), spare
        for i in free:
            addition = min(limit - given[i], max(1, budget * loads[i] // mass), spare)
            given[i] = given[i] + addition
            spare = spare - addition
    return np.array(given)


def noise(own_key, shape, width, bound, pieces=(), held_as=jnp.bfloat16):
    gain = steps_of(own_key, shape, pieces, -0.22, 0.18) if pieces else 1.0
    drawn = jax.random.normal(own_key, shape, jnp.float32) * width * gain
    return jnp.minimum(jnp.maximum(drawn, -bound), bound).astype(held_as)


def setup_inputs(seed: int = 0) -> dict:
    streams_of = jax.random.split(jax.random.key(seed), 12)
    hidden = noise(streams_of[0], (SEQS, D), 1.0, 6.0, ((0, 8),))
    token_slab_keys = jax.random.split(jax.random.fold_in(streams_of[1], 1), SEQS // TOK_DEV)
    token_slab_turns = jax.random.permutation(jax.random.fold_in(streams_of[1], 3), SEQS // TOK_DEV)
    token_slab = jax.vmap(lambda own, number: deal_out(jax.random.fold_in(streams_of[1], 2), own, number, TOK_DEV, DEVICES, 1, CAP, 2))(token_slab_keys, token_slab_turns).reshape((SEQS, 1))
    token_row = plant(ranked_ids(streams_of[2], (SEQS,), SLAB, 2), jax.random.fold_in(streams_of[2], 3), 0, SLAB - 1).astype(jnp.int32)
    slab_owner = jax.random.permutation(streams_of[3], DEVICES).astype(jnp.int32)
    ple_table = noise(streams_of[4], (VOCAB, PLEW), 0.0625, 0.375, ((0, 128),))
    norm_gains = jnp.clip(1.0 + 0.18 * jax.random.normal(streams_of[5], (LAYERS, 3, D), jnp.float32), 0.1, 1.9)
    w_gate = noise(streams_of[6], (LAYERS, D, FF), D ** -0.5, 0.125, ((2, 16),))
    w_up = noise(streams_of[7], (LAYERS, D, FF), D ** -0.5, 0.125, ((2, 16),))
    w_down = noise(streams_of[8], (LAYERS, FF, D), FF ** -0.5, 0.0625, ((1, 16),))
    ple_gate = noise(streams_of[9], (LAYERS, D, PLE), D ** -0.5, 0.125, ((2, 16),))
    ple_proj = noise(streams_of[10], (LAYERS, PLE, D), PLE ** -0.5, 0.375, ((1, 16),))
    return {"hidden": hidden, "token_slab": token_slab, "token_row": token_row, "slab_owner": slab_owner, "ple_table": ple_table, "norm_gains": norm_gains, "w_gate": w_gate, "w_up": w_up, "w_down": w_down, "ple_gate": ple_gate, "ple_proj": ple_proj}


epsilon = 1e-06

def norm_rows(values, scales):
    return values * lax.rsqrt(lax.optimization_barrier(jnp.mean(values * values, axis=-1, keepdims=True)) + epsilon) * scales

def reference(hidden, token_slab, token_row, slab_owner, ple_table, norm_gains, w_gate, w_up, w_down, ple_gate, ple_proj):
    store_index = (slab_owner[token_slab[:, 0]] * SLAB + token_row).astype(jnp.int32)
    looked = jnp.take(ple_table, store_index, axis=0)
    ple_part = looked.astype(jnp.float32).reshape(SEQS, LAYERS, PLE) * PLE ** 0.5
    current = hidden.astype(jnp.float32)
    for layer_at in range(LAYERS):
        normed = norm_rows(current, norm_gains[layer_at, 0]).astype(jnp.bfloat16)
        gate_part = jnp.dot(normed, w_gate[layer_at], preferred_element_type=jnp.float32)
        up_part = jnp.dot(normed, w_up[layer_at], preferred_element_type=jnp.float32)
        activated = (jax.nn.gelu(gate_part, approximate=True) * up_part).astype(jnp.bfloat16)
        mlp_out = jnp.dot(activated, w_down[layer_at], preferred_element_type=jnp.float32)
        current = current + norm_rows(mlp_out, norm_gains[layer_at, 1])
        current_b = current.astype(jnp.bfloat16)
        ple_gate_out = jnp.dot(current_b, ple_gate[layer_at], preferred_element_type=jnp.float32)
        ple_act = (jax.nn.gelu(ple_gate_out, approximate=True) * ple_part[:, layer_at, :]).astype(jnp.bfloat16)
        ple_out = jnp.dot(ple_act, ple_proj[layer_at], preferred_element_type=jnp.float32)
        current = current + norm_rows(ple_out, norm_gains[layer_at, 2])
    return current.astype(jnp.bfloat16)
```

```python
import jax
import jax.numpy as jnp
from jax import lax
from jax.sharding import PartitionSpec as P

PLE = 256
epsilon = 1e-06


def norm_rows(values, scales):
    return values * lax.rsqrt(jnp.mean(values * values, axis=-1, keepdims=True) + epsilon) * scales


def per_device(
    hidden,
    token_slab,
    token_row,
    slab_owner,
    ple_table,
    norm_gains,
    w_gate,
    w_up,
    w_down,
    ple_gate,
    ple_proj,
):
    members = lax.axis_size("member")
    devices = lax.axis_size("group") * members
    tokens_here = token_row.shape[0]
    slots = max(2, (2 * tokens_here + devices - 1) // devices)
    me = lax.axis_index("member")

    gate_full = lax.all_gather(ple_gate[0].T, "member", axis=0, tiled=True)
    proj_full = lax.all_gather(ple_proj[0], "member", axis=0, tiled=True)

    normed = norm_rows(hidden.astype(jnp.float32), norm_gains[0, 0]).astype(jnp.bfloat16)
    gate_part = jnp.dot(normed, w_gate[0], preferred_element_type=jnp.float32)
    up_part = jnp.dot(normed, w_up[0], preferred_element_type=jnp.float32)
    activated = (jax.nn.gelu(gate_part, approximate=True) * up_part).astype(jnp.bfloat16)
    partial = jnp.dot(activated, w_down[0], preferred_element_type=jnp.float32).astype(jnp.bfloat16)
    mlp_out = lax.psum_scatter(partial, "member", scatter_dimension=0, tiled=True).astype(jnp.float32)

    target = slab_owner[token_slab[:, 0]]
    order = jnp.arange(tokens_here, dtype=jnp.int32)
    earlier = (target[None, :] == target[:, None]) & (order[None, :] < order[:, None])
    slot_of = jnp.sum(earlier.astype(jnp.int32), axis=1)
    hit_map = (target[:, None, None] == jnp.arange(devices, dtype=jnp.int32)[None, :, None]) & (
        slot_of[:, None, None] == jnp.arange(slots, dtype=jnp.int32)[None, None, :]
    )
    requests = jnp.sum(jnp.where(hit_map, token_row[:, None, None] + 1, 0), axis=0)
    received = lax.all_to_all(requests, ("group", "member"), split_axis=0, concat_axis=0, tiled=True)
    flat_ids = received.reshape(-1) - 1
    one_hot = (flat_ids[:, None] == jnp.arange(ple_table.shape[0], dtype=jnp.int32)[None, :]).astype(jnp.bfloat16)
    served = jnp.dot(one_hot, ple_table, preferred_element_type=jnp.float32).astype(jnp.bfloat16)
    served = served.reshape(devices, slots * ple_table.shape[1])
    returned = lax.all_to_all(served, ("group", "member"), split_axis=0, concat_axis=0, tiled=True)
    returned = returned.reshape(devices * slots, ple_table.shape[1])
    own_rows = jnp.dot(hit_map.reshape(tokens_here, devices * slots).astype(jnp.bfloat16), returned,
                       preferred_element_type=jnp.float32)

    mine = lax.dynamic_slice_in_dim(hidden, me * tokens_here, tokens_here, 0).astype(jnp.float32)
    current = mine + norm_rows(mlp_out, norm_gains[0, 1])
    current_b = current.astype(jnp.bfloat16)
    gate_out = lax.dot_general(current_b, gate_full, (((1,), (1,)), ((), ())), preferred_element_type=jnp.float32)
    ple_act = (jax.nn.gelu(gate_out, approximate=True) * (own_rows * PLE**0.5)).astype(jnp.bfloat16)
    ple_out = jnp.dot(ple_act, proj_full, preferred_element_type=jnp.float32)
    current = current + norm_rows(ple_out, norm_gains[0, 2])
    return lax.all_gather(current.astype(jnp.bfloat16), "member", axis=0, tiled=True)


def solution(mesh):
    return jax.shard_map(
        per_device,
        mesh=mesh,
        in_specs=(
            P("group", None),
            P(("group", "member"), None),
            P(("group", "member")),
            P(),
            P(("group", "member"), None),
            P(),
            P(None, None, "member"),
            P(None, None, "member"),
            P(None, "member", None),
            P(None, None, "member"),
            P(None, "member", None),
        ),
        out_specs=P("group", None),
        check_vma=False,
    )
```

```python
import functools

import jax
import jax.numpy as jnp
from jax import lax
from jax.experimental import pallas as pl
from jax.experimental.pallas import tpu as pltpu
from jax.sharding import PartitionSpec as P

EPS = 1e-06
MESH = pl.DeviceIdType.MESH
BF, F32 = jnp.bfloat16, jnp.float32
SIDE = 4
GROUPS = (
    ((2, 2), (2, 1), (2, 3), (2, 0)),
    ((0, 2), (1, 2), (3, 2), (1, 1)),
    ((1, 3), (3, 1), (3, 3), (1, 0)),
    ((3, 0), (0, 1), (0, 3), (0, 0)),
)
ORDER = [piece for group in GROUPS for piece in group]


def slot(h, da, db):
    return ORDER.index((da, db) if h == 0 else (db, da))


def gelu(v):
    return 0.5 * v * (1.0 + jnp.tanh(0.7978845608028654 * (v + 0.044715 * (v * v * v))))


def rms_scale(v):
    return lax.rsqrt(jnp.mean(v * v, axis=-1, keepdims=True) + EPS)


def diagonal_column(row, n):
    eye = lax.broadcasted_iota(jnp.int32, (n, n), 0) == lax.broadcasted_iota(jnp.int32, (n, n), 1)
    return jnp.sum(jnp.where(eye, row, 0.0), axis=1, keepdims=True)


def body(
    nz, slab_rows,
    hid_hbm, wg_hbm, wu_hbm, wd_hbm, pg_hbm, pp_hbm, table_hbm, gains, slab, rowid, owner,
    out,
    hid, own, wg, wu, wd, table, act, part, r1a, r1b, r2a, r2b, ids, a0, a1, a2, a3, a4, wb,
    local_sem, ss1a, rs1a, ss1b, rs1b, ss2a, rs2a, ss2b, rs2b, sg1, rg1, sg2, rg2, sg3, rg3, sg4, rg4,
    sid, rid, sw, rw, sx, rx,
):
    tok, d = own.shape
    half, t2 = d // 2, tok // 2
    lanes = wb.shape[-1]
    pw = table.shape[1]
    ndev = nz * 2 * SIDE * SIDE
    g, m = lax.axis_index("group"), lax.axis_index("member")
    z, c = g // 2, lax.rem(g, 2)
    x, y = m // SIDE, lax.rem(m, SIDE)

    def at(dx, dy):
        return lax.rem(x + dx, SIDE) * SIDE + lax.rem(y + dy, SIDE)

    def along(axis, off):
        if axis == "x":
            return (g, at(off, 0))
        if axis == "y":
            return (g, at(0, off))
        if axis == "z":
            return (lax.rem(z + off, nz) * 2 + c, m)
        return (z * 2 + 1 - c, m)

    def send(src, dst, s, r, dev):
        copy = pltpu.make_async_remote_copy(
            src_ref=src, dst_ref=dst, send_sem=s, recv_sem=r, device_id=dev, device_id_type=MESH
        )
        return copy

    sizes = {"y": SIDE, "x": SIDE, "z": nz, "c": 2}
    peers = [(a, o) for a in "yxzc" for o in range(1, sizes[a])]

    locals_ = []

    def local(src, dst):
        copy = pltpu.make_async_copy(src, dst, local_sem.at[len(locals_)])
        copy.start()
        locals_.append(copy)
        return copy

    lane0 = pl.multiple_of(g * lanes, 128)
    hid_in = []
    in_pg = local(pg_hbm.at[:, pl.ds(lane0, lanes)], wb.at[z, c, 0, x, y])
    in_pp = local(pp_hbm.at[:, pl.ds(lane0, lanes)], wb.at[z, c, 1, x, y])
    for k, (dx, dy) in enumerate(ORDER):
        if k == 4:
            in_wg = local(wg_hbm, wg)
            in_wu = local(wu_hbm, wu)
            in_wd = local(wd_hbm, wd)
        hid_in.append(local(hid_hbm.at[at(dx, dy)], hid.at[k]))
    in_own = local(hid_hbm.at[m], own)
    in_table = local(table_hbm, table)

    barrier = pltpu.get_barrier_semaphore()
    for a, o in peers:
        pl.semaphore_signal(barrier, inc=1, device_id=along(a, o), device_id_type=MESH)

    owner_col = diagonal_column(owner[...].astype(F32), ndev)
    slab_row = slab[...]
    match = lax.broadcasted_iota(jnp.int32, (ndev, tok), 0) == slab_row
    target_row = jnp.sum(jnp.where(match, owner_col, 0.0), axis=0, keepdims=True)
    ids[z, c, x, y] = target_row * float(slab_rows) + rowid[...].astype(F32)

    pl.semaphore_wait(barrier, len(peers))

    started = []

    def exchange(ref_of, dst_of, s, r, axis, base):
        copies = []
        for o in range(1, sizes[axis]):
            n = base + o - 1
            copy = send(ref_of(o), dst_of(o), s.at[n], r.at[n], along(axis, o))
            copy.start()
            copies.append(copy)
        started.extend(copies)
        return copies

    base_of = {"y": 0, "x": SIDE - 1, "z": 2 * SIDE - 2, "c": 2 * SIDE - 3 + nz}

    def gather_stage(ref, with_t, s, r, axis):
        if axis == "y":
            view = ref.at[z, c, :, x, y] if with_t else ref.at[z, c, x, y]
        elif axis == "x":
            view = ref.at[z, c, :, x] if with_t else ref.at[z, c, x]
        elif axis == "z":
            view = ref.at[z, c]
        else:
            view = ref.at[:, c]
        return exchange(lambda o: view, lambda o: view, s, r, axis, base_of[axis])

    def arrive(copies):
        for copy in copies:
            copy.wait_recv()

    def gathers(axis):
        return gather_stage(ids, False, sid, rid, axis) + gather_stage(wb, True, sw, rw, axis)

    in_pg.wait()
    in_pp.wait()
    flight = gathers("y")

    m1a, m1b, m2a, m2b = {}, {}, {}, {}
    rows = (slice(0, t2), slice(t2, tok))
    first_axis, second_axis = ("x", "y"), ("y", "x")
    step = (1, SIDE - 1)

    def go(table_, key, src, dst, s, r, dev):
        copy = send(src, dst, s, r, dev)
        copy.start()
        table_[key] = copy
        started.append(copy)

    def send_1b(h, way, db, t):
        da = step[way]
        go(m1b, (h, way, db, t), part.at[h, slot(h, da, db), rows[t]], r1b.at[h, way, db, rows[t]],
           ss1b.at[h, way, db, t], rs1b.at[h, way, db, t], along(first_axis[h], step[way]))

    def send_ready(piece):
        for h in range(2):
            da, db = piece if h == 0 else piece[::-1]
            if da == 2:
                for way in range(2):
                    go(m1a, (h, way, db), part.at[h, slot(h, 2, db), rows[way]], r1a.at[h, way, db],
                       ss1a.at[h, way, db], rs1a.at[h, way, db], along(first_axis[h], step[way]))
            elif da == 1:
                send_1b(h, 0, db, 1)
            elif da == 3:
                send_1b(h, 1, db, 0)

    def compute(gi):
        k0 = gi * 4
        for k in range(k0, k0 + 4):
            hid_in[k].wait()
        gain = gains[0]

        @pl.loop(0, 4)
        def _(i):
            v = hid[k0 + i].astype(F32)
            hid[k0 + i] = (v * rms_scale(v) * gain).astype(BF)

        n = wg.shape[1]
        tile = min(256, n)
        if gi == 0:
            in_wg.wait()
            in_wu.wait()

        @pl.loop(0, n // tile)
        def _(j):
            cols = pl.ds(pl.multiple_of(j * tile, 128), tile)
            v = hid[k0:k0 + 4].reshape(4 * tok, d)
            gate = jnp.dot(v, wg[:, cols], preferred_element_type=F32)
            up = jnp.dot(v, wu[:, cols], preferred_element_type=F32)
            act[:, cols] = (gelu(gate) * up).astype(BF)

        if gi == 0:
            in_wd.wait()
        dt = min(256, half)
        per = half // dt

        @pl.loop(0, 2 * per)
        def _(j):
            cols = pl.ds(pl.multiple_of(j * dt, 128), dt)
            out_cols = pl.ds(pl.multiple_of(lax.rem(j, per) * dt, 128), dt)
            v = jnp.dot(act[...], wd[:, cols], preferred_element_type=F32).astype(BF)
            part[j // per, k0:k0 + 4, :, out_cols] = v.reshape(4, tok, dt)

        for piece in GROUPS[gi]:
            send_ready(piece)

    def add_into(h, k, r, other):
        part[h, k, r] = (part[h, k, r].astype(F32) + other[...].astype(F32)).astype(BF)

    def relay_1b(db):
        for h in range(2):
            for way in range(2):
                m1a[h, way, db].wait_recv()
                add_into(h, slot(h, step[way], db), rows[way], r1a.at[h, way, db])
                send_1b(h, way, db, way)

    compute(0)
    arrive(flight)
    flight = gathers("x")
    compute(1)
    arrive(flight)
    flight = gathers("z")
    compute(2)
    relay_1b(2)
    arrive(flight)
    flight = gathers("c")
    compute(3)
    for db in (1, 3, 0):
        relay_1b(db)
    arrive(flight)

    in_table.wait()
    rel = ids[...].reshape(ndev, tok) - ((g * SIDE * SIDE + m) * slab_rows).astype(F32)
    hit = (rel >= 0.0) & (rel < float(slab_rows))
    lane = lax.broadcasted_iota(jnp.int32, (ndev, tok), 1).astype(F32)
    first = jnp.min(jnp.where(hit, lane, 1e4), axis=1, keepdims=True)
    last = jnp.max(jnp.where(hit, lane, -1.0), axis=1, keepdims=True)
    id0 = jnp.sum(jnp.where(hit & (lane == first), rel, 0.0), axis=1, keepdims=True)
    id1 = jnp.sum(jnp.where(hit & (lane == last), rel, 0.0), axis=1, keepdims=True)
    id0 = jnp.where(first < 5e3, id0, -1.0).astype(jnp.int32)
    id1 = jnp.where(last > first, id1, -1.0).astype(jnp.int32)
    row_iota = lax.broadcasted_iota(jnp.int32, (ndev, slab_rows), 1)
    for i, wanted in enumerate((id0, id1)):
        pick = jnp.where(row_iota == wanted, 1.0, 0.0).astype(BF)
        served = jnp.dot(pick, table[...], preferred_element_type=F32)
        a0[:, :, :, :, :, i * pw:(i + 1) * pw] = served.reshape(nz, 2, SIDE, SIDE, 1, pw)

    def return_c():
        a1[:, c] = a0[:, c]
        return exchange(lambda o: a0.at[:, 1 - c], lambda o: a1.at[:, c], sx, rx, "c", base_of["c"])

    def return_z():
        a2[z] = a1[z]
        return exchange(lambda o: a1.at[lax.rem(z + o, nz)], lambda o: a2.at[z], sx, rx, "z", base_of["z"])

    def return_x():
        a3[:, :, x] = a2[:, :, x]
        return exchange(
            lambda o: a2.at[:, :, lax.rem(x + o, SIDE)], lambda o: a3.at[:, :, x], sx, rx, "x", base_of["x"])

    def return_y():
        a4[:, :, :, y] = a3[:, :, :, y]
        return exchange(
            lambda o: a3.at[:, :, :, lax.rem(y + o, SIDE)], lambda o: a4.at[:, :, :, y], sx, rx, "y", base_of["y"])

    def sum_first(db):
        for h in range(2):
            for way in range(2):
                for t in range(2):
                    m1b[h, way, db, t].wait_recv()
            k = slot(h, 0, db)
            total = part[h, k].astype(F32) + r1b[h, 0, db].astype(F32) + r1b[h, 1, db].astype(F32)
            part[h, k] = total.astype(BF)
            if db == 2:
                for way in range(2):
                    go(m2a, (h, way), part.at[h, k, rows[way]], r2a.at[h, way],
                       ss2a.at[h, way], rs2a.at[h, way], along(second_axis[h], step[way]))
            elif db == 1:
                send_2b(h, 0, 1)
            elif db == 3:
                send_2b(h, 1, 0)

    def send_2b(h, way, t):
        go(m2b, (h, way, t), part.at[h, slot(h, 0, step[way]), rows[t]], r2b.at[h, way, rows[t]],
           ss2b.at[h, way, t], rs2b.at[h, way, t], along(second_axis[h], step[way]))

    flight = return_c()
    sum_first(2)
    arrive(flight)
    flight = return_z()
    sum_first(1)
    arrive(flight)
    flight = return_x()
    sum_first(3)
    for h in range(2):
        for way in range(2):
            m2a[h, way].wait_recv()
            add_into(h, slot(h, 0, step[way]), rows[way], r2a.at[h, way])
            send_2b(h, way, way)
    arrive(flight)
    flight = return_y()
    sum_first(0)
    for h in range(2):
        for way in range(2):
            for t in range(2):
                m2b[h, way, t].wait_recv()

    in_own.wait()
    sums = [
        part[h, slot(h, 0, 0)].astype(F32) + r2b[h, 0].astype(F32) + r2b[h, 1].astype(F32) for h in range(2)
    ]
    mlp = jnp.concatenate(sums, axis=1)
    current = own[...].astype(F32) + mlp * rms_scale(mlp) * gains[1]
    current_b = current.astype(BF)
    nb = nz * 2
    gate = jnp.zeros((tok, SIDE * SIDE * wb.shape[5]), F32)
    for b in range(nb):
        w = wb[b // 2, b % 2, 0].reshape(SIDE * SIDE * wb.shape[5], lanes)
        gate += lax.dot_general(
            current_b[:, b * lanes:(b + 1) * lanes], w, (((1,), (1,)), ((), ())), preferred_element_type=F32)

    arrive(flight)
    target_col = diagonal_column(target_row, tok)
    i0 = lax.broadcasted_iota(jnp.int32, (tok, tok), 0)
    i1 = lax.broadcasted_iota(jnp.int32, (tok, tok), 1)
    second = jnp.max(jnp.where((target_col == target_row) & (i1 < i0), 1.0, 0.0), axis=1, keepdims=True)
    owners = lax.broadcasted_iota(jnp.int32, (tok, ndev), 1).astype(F32) == target_col
    looked = jnp.zeros((tok, pw), F32)
    for i in range(2):
        pick = jnp.where(owners & (second == float(i)), 1.0, 0.0).astype(BF)
        rows_i = a4[:, :, :, :, :, i * pw:(i + 1) * pw].reshape(ndev, pw).astype(BF)
        looked += jnp.dot(pick, rows_i, preferred_element_type=F32)
    ple_act = (gelu(gate) * (looked * float(pw) ** 0.5)).astype(BF)
    ple = jnp.concatenate(
        [
            jnp.dot(ple_act, wb[b // 2, b % 2, 1].reshape(SIDE * SIDE * wb.shape[5], lanes),
                    preferred_element_type=F32)
            for b in range(nb)
        ],
        axis=1,
    )
    out[m] = (current + ple * rms_scale(ple) * gains[2]).astype(BF)

    cols = (slice(0, half), slice(half, d))
    g1, g2, g3, g4 = {}, {}, {}, {}

    def member(h, da, db):
        return at(da, db) if h == 0 else at(db, da)

    def spread(h, db):
        for way in range(2):
            view = out.at[member(h, 0, db), :, cols[h]]
            go(g3, (h, way, db), view, view, sg3.at[h, way, db], rg3.at[h, way, db],
               along(first_axis[h], step[way]))

    for h in range(2):
        for way in range(2):
            view = out.at[m, :, cols[h]]
            go(g1, (h, way), view, view, sg1.at[h, way], rg1.at[h, way], along(second_axis[h], step[way]))
    for h in range(2):
        spread(h, 0)
    for way in range(2):
        for h in range(2):
            g1[h, way].wait_recv()
            view = out.at[member(h, 0, step[1 - way]), rows[way], cols[h]]
            go(g2, (h, way), view, view, sg2.at[h, way], rg2.at[h, way], along(second_axis[h], step[way]))
    for db in (1, 3):
        for h in range(2):
            spread(h, db)

    def forward(db):
        for h in range(2):
            for way in range(2):
                g3[h, way, db].wait_recv()
                view = out.at[member(h, step[1 - way], db), rows[way], cols[h]]
                go(g4, (h, way, db), view, view, sg4.at[h, way, db], rg4.at[h, way, db],
                   along(first_axis[h], step[way]))

    for h in range(2):
        for way in range(2):
            g2[h, way].wait_recv()
        spread(h, 2)
    for db in (0, 1, 3, 2):
        forward(db)
    for copy in g4.values():
        copy.wait_recv()
    for copy in started:
        copy.wait_send()


def per_device(
    hidden, token_slab, token_row, slab_owner, ple_table, norm_gains, w_gate, w_up, w_down, ple_gate, ple_proj
):
    members = lax.axis_size("member")
    nz = lax.axis_size("group") // 2
    tok = token_row.shape[0]
    d, n = w_gate.shape[1:]
    slab_rows, pw = ple_table.shape
    half, t2 = d // 2, tok // 2
    per = ple_gate.shape[2]
    lanes = d // (2 * nz)
    dma = pltpu.SemaphoreType.DMA
    anyspace, vmem = pl.BlockSpec(memory_space=pl.ANY), pl.BlockSpec(memory_space=pltpu.VMEM)
    stages = 2 * (SIDE - 1) + nz
    rows_buf = pltpu.VMEM((nz, 2, SIDE, SIDE, 1, 2 * pw), F32)
    pairs = [(2, 2, 4), (2, 2, 4, 2), (2, 2), (2, 2, 2), (2, 2), (2, 2), (2, 2, 4), (2, 2, 4), (stages,), (stages,), (stages,)]
    call = pl.pallas_call(
        functools.partial(body, nz, slab_rows),
        out_shape=jax.ShapeDtypeStruct((members, tok, d), BF),
        in_specs=[anyspace] * 7 + [vmem] * 4,
        out_specs=vmem,
        scratch_shapes=[
            pltpu.VMEM((16, tok, d), BF),
            pltpu.VMEM((tok, d), BF),
            pltpu.VMEM((d, n), BF),
            pltpu.VMEM((d, n), BF),
            pltpu.VMEM((n, d), BF),
            pltpu.VMEM((slab_rows, pw), BF),
            pltpu.VMEM((4 * tok, n), BF),
            pltpu.VMEM((2, 16, tok, half), BF),
            pltpu.VMEM((2, 2, 4, t2, half), BF),
            pltpu.VMEM((2, 2, 4, tok, half), BF),
            pltpu.VMEM((2, 2, t2, half), BF),
            pltpu.VMEM((2, 2, tok, half), BF),
            pltpu.VMEM((nz, 2, SIDE, SIDE, 1, tok), F32),
            rows_buf, rows_buf, rows_buf, rows_buf, rows_buf,
            pltpu.VMEM((nz, 2, 2, SIDE, SIDE, per, lanes), BF),
            dma((24,)),
        ] + [dma(shape) for shape in pairs for _ in range(2)],
        compiler_params=pltpu.CompilerParams(
            collective_id=0, has_side_effects=True, vmem_limit_bytes=60 * 1024 * 1024
        ),
        name="layer",
    )
    out = call(
        hidden.reshape(members, tok, d), w_gate[0], w_up[0], w_down[0], ple_gate[0].T, ple_proj[0], ple_table,
        norm_gains.reshape(3, 1, d), token_slab.reshape(1, tok), token_row.reshape(1, tok),
        slab_owner.reshape(1, -1),
    )
    return out.reshape(members * tok, d)


def solution(mesh):
    return jax.shard_map(
        per_device,
        mesh=mesh,
        in_specs=(
            P("group", None),
            P(("group", "member"), None),
            P(("group", "member")),
            P(),
            P(("group", "member"), None),
            P(),
            P(None, None, "member"),
            P(None, None, "member"),
            P(None, "member", None),
            P(None, None, "member"),
            P(None, "member", None),
        ),
        out_specs=P("group", None),
        check_vma=False,
    )
```

```python
import functools

import jax
import jax.numpy as jnp
from jax import lax
from jax.experimental import pallas as pl
from jax.experimental.pallas import tpu as pltpu
from jax.sharding import PartitionSpec as P

EPS = 1e-06
MESH = pl.DeviceIdType.MESH
BF, F32 = jnp.bfloat16, jnp.float32
SIDE = 4
ORDER = [
    (2, 2), (1, 2), (2, 1), (3, 2), (2, 3),
    (1, 1), (1, 3), (3, 1), (3, 3), (0, 2), (2, 0),
    (0, 1), (1, 0), (0, 3), (3, 0), (0, 0),
]
SPLITS = ((0, 5, 11, 16), (0, 8, 16))
WAVES = (2, 1, 3, 0)


def slot(h, da, db):
    return ORDER.index((da, db) if h == 0 else (db, da))


def gelu(v):
    return 0.5 * v * (1.0 + jnp.tanh(0.7978845608028654 * (v + 0.044715 * (v * v * v))))


def rms_scale(v):
    return lax.rsqrt(jnp.mean(v * v, axis=-1, keepdims=True) + EPS)


def diagonal_column(row, n):
    eye = lax.broadcasted_iota(jnp.int32, (n, n), 0) == lax.broadcasted_iota(jnp.int32, (n, n), 1)
    return jnp.sum(jnp.where(eye, row, 0.0), axis=1, keepdims=True)


def body(
    nz, slab_rows,
    hid_hbm, wg_hbm, wu_hbm, wd_hbm, pg_hbm, pp_hbm, table_hbm, gains_hbm, slab_hbm, rowid_hbm, owner_hbm,
    out,
    hid, own, wg, wu, wd, table, act, part, r1a, r1b, r2a, r2b, ids, a0, a1, a2, a3, a4, wb,
    gains, slab, rowid, owner, looked,
    local_sem, ss1a, rs1a, ss1b, rs1b, ss2a, rs2a, ss2b, rs2b, sg1, rg1, sg2, rg2, sg3, rg3, sg4, rg4,
    sid, rid, sw, rw, sx, rx,
):
    tok, d = own.shape
    half, tq = d // 2, tok // 2
    quarter = half // 2
    lanes = wb.shape[-1]
    pw = table.shape[1]
    ndev = nz * 2 * SIDE * SIDE
    g, m = lax.axis_index("group"), lax.axis_index("member")
    z, c = g // 2, lax.rem(g, 2)
    x, y = m // SIDE, lax.rem(m, SIDE)
    toks = (slice(0, tq), slice(tq, tok))
    sub = (slice(0, quarter), slice(quarter, half))
    first_axis, second_axis = ("x", "y"), ("y", "x")
    step = (1, SIDE - 1)

    def at(dx, dy):
        return lax.rem(x + dx, SIDE) * SIDE + lax.rem(y + dy, SIDE)

    def along(axis, off):
        if axis == "x":
            return (g, at(off, 0))
        if axis == "y":
            return (g, at(0, off))
        if axis == "z":
            return (lax.rem(z + off, nz) * 2 + c, m)
        return (z * 2 + 1 - c, m)

    sizes = {"y": SIDE, "x": SIDE, "z": nz, "c": 2}
    peers = [(a, o) for a in "yxzc" for o in range(1, sizes[a])]

    barrier = pltpu.get_barrier_semaphore()
    for a, o in peers:
        pl.semaphore_signal(barrier, inc=1, device_id=along(a, o), device_id_type=MESH)

    locals_ = []

    def local(src, dst):
        copy = pltpu.make_async_copy(src, dst, local_sem.at[len(locals_)])
        copy.start()
        locals_.append(copy)
        return copy

    in_small = [local(owner_hbm, owner), local(slab_hbm, slab), local(rowid_hbm, rowid)]
    in_gains = local(gains_hbm, gains)
    hid_in = {}

    def load_hidden(q, k0, k1):
        for k in range(k0, k1):
            hid_in[q, k] = local(hid_hbm.at[at(*ORDER[k]), toks[q]], hid.at[q, k])

    load_hidden(0, 0, 5)
    lane0 = pl.multiple_of(g * lanes, 128)
    in_w = [
        local(pg_hbm.at[:, pl.ds(lane0, lanes)], wb.at[z, c, 0, x, y]),
        local(pp_hbm.at[:, pl.ds(lane0, lanes)], wb.at[z, c, 1, x, y]),
    ]
    in_wg = local(wg_hbm, wg)
    in_wu = local(wu_hbm, wu)
    in_wd = local(wd_hbm, wd)
    load_hidden(0, 5, 16)
    load_hidden(1, 0, 16)
    in_table = local(table_hbm, table)
    in_own = local(hid_hbm.at[m], own)

    for copy in in_small:
        copy.wait()
    owner_col = diagonal_column(owner[...].astype(F32), ndev)
    match = lax.broadcasted_iota(jnp.int32, (ndev, tok), 0) == slab[...]
    target_row = jnp.sum(jnp.where(match, owner_col, 0.0), axis=0, keepdims=True)
    ids[z, c, x, y] = target_row * float(slab_rows) + rowid[...].astype(F32)

    pl.semaphore_wait(barrier, len(peers))

    started = []

    def launch(src, dst, s, r, dev):
        copy = pltpu.make_async_remote_copy(
            src_ref=src, dst_ref=dst, send_sem=s, recv_sem=r, device_id=dev, device_id_type=MESH
        )
        copy.start()
        started.append(copy)
        return copy

    base = {"y": 0, "x": SIDE - 1, "z": 2 * SIDE - 2, "c": 2 * SIDE - 3 + nz}

    def exchange(ref_of, dst, s, r, axis):
        return [
            launch(ref_of(o), dst, s.at[base[axis] + o - 1], r.at[base[axis] + o - 1], along(axis, o))
            for o in range(1, sizes[axis])
        ]

    def arrive(copies):
        for copy in copies:
            copy.wait_recv()

    def gather_ids(axis):
        view = {"y": lambda: ids.at[z, c, x, y], "x": lambda: ids.at[z, c, x], "z": lambda: ids.at[z, c],
                "c": lambda: ids.at[:, c]}[axis]()
        return exchange(lambda o: view, view, sid, rid, axis)

    def gather_w(axis):
        view = {"y": lambda: wb.at[z, c, :, x, y], "x": lambda: wb.at[z, c, :, x], "z": lambda: wb.at[z, c],
                "c": lambda: wb.at[:, c]}[axis]()
        return exchange(lambda o: view, view, sw, rw, axis)

    m1a, m1b, m2a, m2b = {}, {}, {}, {}

    def send_1a(h, q, way, db):
        m1a[h, q, way, db] = launch(
            part.at[h, q, slot(h, 2, db), :, sub[way]], r1a.at[h, q, way, db],
            ss1a.at[h, q, way, db], rs1a.at[h, q, way, db], along(first_axis[h], step[way]))

    def send_1b(h, q, way, db, t):
        m1b[h, q, way, db, t] = launch(
            part.at[h, q, slot(h, step[way], db), :, sub[t]], r1b.at[h, q, way, db, :, sub[t]],
            ss1b.at[h, q, way, db, t], rs1b.at[h, q, way, db, t], along(first_axis[h], step[way]))

    def send_2a(h, q, way):
        m2a[h, q, way] = launch(
            part.at[h, q, slot(h, 0, 2), :, sub[way]], r2a.at[h, q, way],
            ss2a.at[h, q, way], rs2a.at[h, q, way], along(second_axis[h], step[way]))

    def send_2b(h, q, way, t):
        m2b[h, q, way, t] = launch(
            part.at[h, q, slot(h, 0, step[way]), :, sub[t]], r2b.at[h, q, way, :, sub[t]],
            ss2b.at[h, q, way, t], rs2b.at[h, q, way, t], along(second_axis[h], step[way]))

    def send_ready(q, i):
        todo = sorted(
            (WAVES.index(db), h, da, db)
            for h in range(2)
            for da, db in (p if h == 0 else p[::-1] for p in ORDER[SPLITS[q][i]:SPLITS[q][i + 1]])
        )
        for _, h, da, db in todo:
            if da == 2:
                for way in range(2):
                    send_1a(h, q, way, db)
        for _, h, da, db in todo:
            if da in (1, 3):
                way = step.index(da)
                send_1b(h, q, way, db, 1 - way)

    def compute(q, i, between=lambda: None):
        k0, k1 = SPLITS[q][i], SPLITS[q][i + 1]
        rows = (k1 - k0) * tq
        for k in range(k0, k1):
            hid_in[q, k].wait()
        if (q, i) == (0, 0):
            in_gains.wait()
        gain = gains[0]

        @pl.loop(0, k1 - k0)
        def _(k):
            v = hid[q, k0 + k].astype(F32)
            hid[q, k0 + k] = (v * rms_scale(v) * gain).astype(BF)

        n = wg.shape[1]
        tile = min(256, n)
        if (q, i) == (0, 0):
            in_wg.wait()
            in_wu.wait()

        @pl.loop(0, n // tile)
        def _(j):
            cols = pl.ds(pl.multiple_of(j * tile, 128), tile)
            v = hid[q, k0:k1].reshape(rows, d)
            gate = jnp.dot(v, wg[:, cols], preferred_element_type=F32)
            up = jnp.dot(v, wu[:, cols], preferred_element_type=F32)
            act[0:rows, cols] = (gelu(gate) * up).astype(BF)

        between()
        if (q, i) == (0, 0):
            in_wd.wait()
        dt = min(256, half)
        per = half // dt

        @pl.loop(0, 2 * per)
        def _(j):
            cols = pl.ds(pl.multiple_of(j * dt, 128), dt)
            out_cols = pl.ds(pl.multiple_of(lax.rem(j, per) * dt, 128), dt)
            v = jnp.dot(act[0:rows, :], wd[:, cols], preferred_element_type=F32).astype(BF)
            part[j // per, q, k0:k1, :, out_cols] = v.reshape(k1 - k0, tq, dt)

    def add_into(h, q, k, t, other):
        part[h, q, k, :, sub[t]] = (part[h, q, k, :, sub[t]].astype(F32) + other[...].astype(F32)).astype(BF)

    def relay_1(q, db):
        for h in range(2):
            for way in range(2):
                m1a[h, q, way, db].wait_recv()
                add_into(h, q, slot(h, step[way], db), way, r1a.at[h, q, way, db])
                send_1b(h, q, way, db, way)

    def sum_1(q, db):
        for h in range(2):
            for way in range(2):
                for t in range(2):
                    m1b[h, q, way, db, t].wait_recv()
            k = slot(h, 0, db)
            total = part[h, q, k].astype(F32) + r1b[h, q, 0, db].astype(F32) + r1b[h, q, 1, db].astype(F32)
            part[h, q, k] = total.astype(BF)
            if db == 2:
                for way in range(2):
                    send_2a(h, q, way)
            elif db in (1, 3):
                way = step.index(db)
                send_2b(h, q, way, 1 - way)

    def relay_2(q):
        for h in range(2):
            for way in range(2):
                m2a[h, q, way].wait_recv()
                add_into(h, q, slot(h, 0, step[way]), way, r2a.at[h, q, way])
                send_2b(h, q, way, way)

    def serve():
        in_table.wait()
        rel = ids[...].reshape(ndev, tok) - ((g * SIDE * SIDE + m) * slab_rows).astype(F32)
        hit = (rel >= 0.0) & (rel < float(slab_rows))
        lane = lax.broadcasted_iota(jnp.int32, (ndev, tok), 1).astype(F32)
        first = jnp.min(jnp.where(hit, lane, 1e4), axis=1, keepdims=True)
        last = jnp.max(jnp.where(hit, lane, -1.0), axis=1, keepdims=True)
        id0 = jnp.sum(jnp.where(hit & (lane == first), rel, 0.0), axis=1, keepdims=True)
        id1 = jnp.sum(jnp.where(hit & (lane == last), rel, 0.0), axis=1, keepdims=True)
        id0 = jnp.where(first < 5e3, id0, -1.0).astype(jnp.int32)
        id1 = jnp.where(last > first, id1, -1.0).astype(jnp.int32)
        row_iota = lax.broadcasted_iota(jnp.int32, (ndev, slab_rows), 1)
        for i, wanted in enumerate((id0, id1)):
            pick = jnp.where(row_iota == wanted, 1.0, 0.0).astype(BF)
            served = jnp.dot(pick, table[...], preferred_element_type=F32)
            a0[:, :, :, :, :, i * pw:(i + 1) * pw] = served.reshape(nz, 2, SIDE, SIDE, 1, pw)

    def return_c():
        a1[:, c] = a0[:, c]
        return exchange(lambda o: a0.at[:, 1 - c], a1.at[:, c], sx, rx, "c")

    def return_z():
        a2[z] = a1[z]
        return exchange(lambda o: a1.at[lax.rem(z + o, nz)], a2.at[z], sx, rx, "z")

    def return_x():
        a3[:, :, x] = a2[:, :, x]
        return exchange(lambda o: a2.at[:, :, lax.rem(x + o, SIDE)], a3.at[:, :, x], sx, rx, "x")

    def return_y():
        a4[:, :, :, y] = a3[:, :, :, y]
        return exchange(lambda o: a3.at[:, :, :, lax.rem(y + o, SIDE)], a4.at[:, :, :, y], sx, rx, "y")

    def look():
        target_col = diagonal_column(target_row, tok)
        i0 = lax.broadcasted_iota(jnp.int32, (tok, tok), 0)
        i1 = lax.broadcasted_iota(jnp.int32, (tok, tok), 1)
        second = jnp.max(jnp.where((target_col == target_row) & (i1 < i0), 1.0, 0.0), axis=1, keepdims=True)
        owners = lax.broadcasted_iota(jnp.int32, (tok, ndev), 1).astype(F32) == target_col
        rows = jnp.zeros((tok, pw), F32)
        for i in range(2):
            pick = jnp.where(owners & (second == float(i)), 1.0, 0.0).astype(BF)
            rows_i = a4[:, :, :, :, :, i * pw:(i + 1) * pw].reshape(ndev, pw).astype(BF)
            rows += jnp.dot(pick, rows_i, preferred_element_type=F32)
        looked[...] = rows * float(pw) ** 0.5

    nb = nz * 2
    channels = SIDE * SIDE * wb.shape[5]

    def finish(q):
        for h in range(2):
            for way in range(2):
                for t in range(2):
                    m2b[h, q, way, t].wait_recv()
        sums = [
            part[h, q, slot(h, 0, 0)].astype(F32) + r2b[h, q, 0].astype(F32) + r2b[h, q, 1].astype(F32)
            for h in range(2)
        ]
        mlp = jnp.concatenate(sums, axis=1)
        current = own[toks[q]].astype(F32) + mlp * rms_scale(mlp) * gains[1]
        current_b = current.astype(BF)
        gate = jnp.zeros((tq, channels), F32)
        for b in range(nb):
            w = wb[b // 2, b % 2, 0].reshape(channels, lanes)
            gate += lax.dot_general(
                current_b[:, b * lanes:(b + 1) * lanes], w, (((1,), (1,)), ((), ())), preferred_element_type=F32)
        ple_act = (gelu(gate) * looked[toks[q]]).astype(BF)
        ple = jnp.concatenate(
            [
                jnp.dot(ple_act, wb[b // 2, b % 2, 1].reshape(channels, lanes), preferred_element_type=F32)
                for b in range(nb)
            ],
            axis=1,
        )
        out[m, toks[q]] = (current + ple * rms_scale(ple) * gains[2]).astype(BF)

    g1, g2, g3, g4 = {}, {}, {}, {}

    def piece(h, q, da, db, t=None):
        lo = h * half + (0 if t is None else t * quarter)
        width = half if t is None else quarter
        return out.at[at(da, db) if h == 0 else at(db, da), toks[q], lo:lo + width]

    def publish(q):
        for h in range(2):
            for way in range(2):
                view = piece(h, q, 0, 0)
                g1[h, q, way] = launch(view, view, sg1.at[h, q, way], rg1.at[h, q, way],
                                       along(second_axis[h], step[way]))

    def spread(q, db):
        for h in range(2):
            for way in range(2):
                view = piece(h, q, 0, db)
                g3[h, q, way, db] = launch(view, view, sg3.at[h, q, way, db], rg3.at[h, q, way, db],
                                           along(first_axis[h], step[way]))

    def pass_on(q):
        for way in range(2):
            for h in range(2):
                g1[h, q, way].wait_recv()
                view = piece(h, q, 0, step[1 - way], way)
                g2[h, q, way] = launch(view, view, sg2.at[h, q, way], rg2.at[h, q, way],
                                       along(second_axis[h], step[way]))

    def settle(q):
        for h in range(2):
            for way in range(2):
                g2[h, q, way].wait_recv()

    def forward(q, db):
        for h in range(2):
            for way in range(2):
                g3[h, q, way, db].wait_recv()
                view = piece(h, q, step[1 - way], db, way)
                g4[h, q, way, db] = launch(view, view, sg4.at[h, q, way, db], rg4.at[h, q, way, db],
                                           along(first_axis[h], step[way]))

    fi = gather_ids("y")
    for copy in in_w:
        copy.wait()
    fw = gather_w("y")
    box = {}

    def early():
        arrive(fi)
        box["i"] = gather_ids("x")
        arrive(fw)
        box["w"] = gather_w("x")

    compute(0, 0, early)
    send_ready(0, 0)
    compute(0, 1)
    send_ready(0, 1)
    relay_1(0, 2)
    arrive(box["i"])
    fi = gather_ids("z")
    arrive(box["w"])
    fw = gather_w("z")
    compute(0, 2)
    send_ready(0, 2)
    relay_1(0, 1)
    relay_1(0, 3)
    relay_1(0, 0)
    arrive(fi)
    fi = gather_ids("c")
    compute(1, 0)
    sum_1(0, 2)
    send_ready(1, 0)
    arrive(fi)
    serve()
    fx = return_c()
    compute(1, 1)
    sum_1(0, 1)
    sum_1(0, 3)
    arrive(fx)
    fx = return_z()
    relay_2(0)
    send_ready(1, 1)
    relay_1(1, 2)
    arrive(fx)
    fx = return_x()
    relay_1(1, 1)
    relay_1(1, 3)
    relay_1(1, 0)
    arrive(fw)
    fw = gather_w("c")
    sum_1(0, 0)
    arrive(fx)
    fx = return_y()
    sum_1(1, 2)
    arrive(fx)
    in_own.wait()
    look()
    arrive(fw)
    finish(0)
    publish(0)
    spread(0, 0)
    sum_1(1, 1)
    sum_1(1, 3)
    relay_2(1)
    pass_on(0)
    spread(0, 1)
    spread(0, 3)
    sum_1(1, 0)
    settle(0)
    spread(0, 2)
    finish(1)
    publish(1)
    spread(1, 0)
    forward(0, 0)
    pass_on(1)
    spread(1, 1)
    spread(1, 3)
    forward(0, 1)
    forward(0, 3)
    settle(1)
    spread(1, 2)
    forward(0, 2)
    for db in (0, 1, 3, 2):
        forward(1, db)
    arrive(g4.values())
    for copy in started:
        copy.wait_send()


def per_device(
    hidden, token_slab, token_row, slab_owner, ple_table, norm_gains, w_gate, w_up, w_down, ple_gate, ple_proj
):
    members = lax.axis_size("member")
    nz = lax.axis_size("group") // 2
    tok = token_row.shape[0]
    d, n = w_gate.shape[1:]
    slab_rows, pw = ple_table.shape
    half, tq = d // 2, tok // 2
    per = ple_gate.shape[2]
    lanes = d // (2 * nz)
    dma = pltpu.SemaphoreType.DMA
    hbm, vmem = pl.BlockSpec(memory_space=pltpu.HBM), pl.BlockSpec(memory_space=pltpu.VMEM)
    stages = 2 * (SIDE - 1) + nz
    most = max(b - a for split in SPLITS for a, b in zip(split, split[1:]))
    rows_buf = pltpu.VMEM((nz, 2, SIDE, SIDE, 1, 2 * pw), F32)
    pairs = [
        (2, 2, 2, 4), (2, 2, 2, 4, 2), (2, 2, 2), (2, 2, 2, 2),
        (2, 2, 2), (2, 2, 2), (2, 2, 2, 4), (2, 2, 2, 4),
        (stages,), (stages,), (stages,),
    ]
    call = pl.pallas_call(
        functools.partial(body, nz, slab_rows),
        out_shape=jax.ShapeDtypeStruct((members, tok, d), BF),
        in_specs=[hbm] * 11,
        out_specs=vmem,
        scratch_shapes=[
            pltpu.VMEM((2, 16, tq, d), BF),
            pltpu.VMEM((tok, d), BF),
            pltpu.VMEM((d, n), BF),
            pltpu.VMEM((d, n), BF),
            pltpu.VMEM((n, d), BF),
            pltpu.VMEM((slab_rows, pw), BF),
            pltpu.VMEM((most * tq, n), BF),
            pltpu.VMEM((2, 2, 16, tq, half), BF),
            pltpu.VMEM((2, 2, 2, 4, tq, half // 2), BF),
            pltpu.VMEM((2, 2, 2, 4, tq, half), BF),
            pltpu.VMEM((2, 2, 2, tq, half // 2), BF),
            pltpu.VMEM((2, 2, 2, tq, half), BF),
            pltpu.VMEM((nz, 2, SIDE, SIDE, 1, tok), F32),
            rows_buf, rows_buf, rows_buf, rows_buf, rows_buf,
            pltpu.VMEM((nz, 2, 2, SIDE, SIDE, per, lanes), BF),
            pltpu.VMEM((3, 1, d), F32),
            pltpu.VMEM((1, tok), jnp.int32),
            pltpu.VMEM((1, tok), jnp.int32),
            pltpu.VMEM((1, slab_owner.shape[0]), jnp.int32),
            pltpu.VMEM((tok, pw), F32),
            dma((48,)),
        ] + [dma(shape) for shape in pairs for _ in range(2)],
        compiler_params=pltpu.CompilerParams(
            collective_id=0, has_side_effects=True, vmem_limit_bytes=40 * 1024 * 1024
        ),
        name="layer",
    )
    operands = (
        hidden.reshape(members, tok, d), w_gate[0], w_up[0], w_down[0], ple_gate[0].T, ple_proj[0], ple_table,
        norm_gains.reshape(3, 1, d), token_slab.reshape(1, tok), token_row.reshape(1, tok),
        slab_owner.reshape(1, -1),
    )
    out = call(*[pltpu.with_memory_space_constraint(v, pltpu.HBM) for v in operands])
    return out.reshape(members * tok, d)


def solution(mesh):
    return jax.shard_map(
        per_device,
        mesh=mesh,
        in_specs=(
            P("group", None),
            P(("group", "member"), None),
            P(("group", "member")),
            P(),
            P(("group", "member"), None),
            P(),
            P(None, None, "member"),
            P(None, None, "member"),
            P(None, "member", None),
            P(None, None, "member"),
            P(None, "member", None),
        ),
        out_specs=P("group", None),
        check_vma=False,
    )
```

```python
import functools

import jax
import jax.numpy as jnp
from jax import lax
from jax.experimental import pallas as pl
from jax.experimental.pallas import tpu as pltpu
from jax.sharding import PartitionSpec as P

EPS = 1e-06
MESH = pl.DeviceIdType.MESH
BF, F32 = jnp.bfloat16, jnp.float32
SIDE = 4
ORDER = [
    (2, 2), (1, 2), (2, 1), (3, 2), (2, 3),
    (1, 1), (1, 3), (3, 1), (3, 3), (0, 2), (2, 0),
    (0, 1), (1, 0), (0, 3), (3, 0), (0, 0),
]
SPLITS = ((0, 5, 11, 16), (0, 8, 16))
DT = 1024
WAVES = (2, 1, 3, 0)


def slot(h, da, db):
    return ORDER.index((da, db) if h == 0 else (db, da))


def gelu(v):
    return 0.5 * v * (1.0 + jnp.tanh(0.7978845608028654 * (v + 0.044715 * (v * v * v))))


def rms_scale(v):
    return lax.rsqrt(jnp.mean(v * v, axis=-1, keepdims=True) + EPS)


def diagonal_column(row, n):
    eye = lax.broadcasted_iota(jnp.int32, (n, n), 0) == lax.broadcasted_iota(jnp.int32, (n, n), 1)
    return jnp.sum(jnp.where(eye, row, 0.0), axis=1, keepdims=True)


def body(
    nz, slab_rows,
    hid_hbm, wg_hbm, wu_hbm, wd_hbm, pg_hbm, pp_hbm, table_hbm, gains_hbm, slab_hbm, rowid_hbm, owner_hbm,
    out,
    hid, own, wg, wu, wd, table, act, part, r1a, r1b, r2a, r2b, ids, a0, a1, a2, wb,
    gains, slab, rowid, owner, looked,
    local_sem, ss1a, rs1a, ss1b, rs1b, ss2a, rs2a, ss2b, rs2b, sg1, rg1, sg2, rg2, sg3, rg3, sg4, rg4,
    sid, rid, sw, rw, sx, rx,
):
    tok, d = own.shape
    half, tq = d // 2, tok // 2
    quarter = half // 2
    lanes = wb.shape[-1]
    pw = table.shape[1]
    ndev = nz * 2 * SIDE * SIDE
    g, m = lax.axis_index("group"), lax.axis_index("member")
    z, c = g // 2, lax.rem(g, 2)
    x, y = m // SIDE, lax.rem(m, SIDE)
    toks = (slice(0, tq), slice(tq, tok))
    sub = (slice(0, quarter), slice(quarter, half))
    first_axis, second_axis = ("x", "y"), ("y", "x")
    step = (1, SIDE - 1)

    def at(dx, dy):
        return lax.rem(x + dx, SIDE) * SIDE + lax.rem(y + dy, SIDE)

    def along(axis, off):
        if axis == "x":
            return (g, at(off, 0))
        if axis == "y":
            return (g, at(0, off))
        if axis == "z":
            return (lax.rem(z + off, nz) * 2 + c, m)
        return (z * 2 + 1 - c, m)

    shifts = [(dx, dy) for dx in range(SIDE) for dy in range(SIDE) if dx or dy]
    members = [(g, at(dx, dy)) for dx, dy in shifts]
    groups = [(lax.rem(g + o, 2 * nz), m) for o in range(1, 2 * nz)]
    peers = members + groups

    barrier = pltpu.get_barrier_semaphore()
    for peer in peers:
        pl.semaphore_signal(barrier, inc=1, device_id=peer, device_id_type=MESH)

    locals_ = []

    def local(src, dst):
        copy = pltpu.make_async_copy(src, dst, local_sem.at[len(locals_)])
        copy.start()
        locals_.append(copy)
        return copy

    in_small = [local(owner_hbm, owner), local(slab_hbm, slab), local(rowid_hbm, rowid)]
    in_gains = local(gains_hbm, gains)
    hid_in = {}

    def load_hidden(q, k0, k1):
        for k in range(k0, k1):
            hid_in[q, k] = local(hid_hbm.at[at(*ORDER[k]), toks[q]], hid.at[q, k])

    load_hidden(0, 0, 5)
    lane0 = pl.multiple_of(g * lanes, 128)
    in_w = [
        local(pg_hbm.at[:, pl.ds(lane0, lanes)], wb.at[z, c, 0, x, y]),
        local(pp_hbm.at[:, pl.ds(lane0, lanes)], wb.at[z, c, 1, x, y]),
    ]
    in_wg = local(wg_hbm, wg)
    in_wu = local(wu_hbm, wu)
    in_wd = local(wd_hbm, wd)
    load_hidden(0, 5, 16)
    load_hidden(1, 0, 16)
    in_table = local(table_hbm, table)
    in_own = local(hid_hbm.at[m], own)

    for copy in in_small:
        copy.wait()
    owner_col = diagonal_column(owner[...].astype(F32), ndev)
    match = lax.broadcasted_iota(jnp.int32, (ndev, tok), 0) == slab[...]
    target_row = jnp.sum(jnp.where(match, owner_col, 0.0), axis=0, keepdims=True)
    ids[z, c, x, y] = target_row * float(slab_rows) + rowid[...].astype(F32)

    pl.semaphore_wait(barrier, len(peers))

    started = []

    def launch(src, dst, s, r, dev):
        copy = pltpu.make_async_remote_copy(
            src_ref=src, dst_ref=dst, send_sem=s, recv_sem=r, device_id=dev, device_id_type=MESH
        )
        copy.start()
        started.append(copy)
        return copy

    def exchange(devices, ref_of, dst, s, r, base):
        return [
            launch(ref_of(*device), dst, s.at[base + i], r.at[base + i], device) for i, device in enumerate(devices)
        ]

    def arrive(copies):
        for copy in copies:
            copy.wait_recv()

    nm, ng = len(members), len(groups)

    def same(devices, view, s, r, base):
        return exchange(devices, lambda *_: view, view, s, r, base)

    def gather_ids(stage):
        if stage == 0:
            return same(members, ids.at[z, c, x, y], sid, rid, 0)
        return same(groups, ids.at[z, c], sid, rid, nm)

    def gather_w(stage):
        if stage == 0:
            return same(members, wb.at[z, c, :, x, y], sw, rw, 0)
        if stage == 1:
            return same([along("z", o) for o in range(1, nz)], wb.at[z, c], sw, rw, nm)
        return same([along("c", 1)], wb.at[:, c], sw, rw, nm + nz - 1)

    m1a, m1b, m2a, m2b = {}, {}, {}, {}

    def send_1a(h, q, way, db):
        m1a[h, q, way, db] = launch(
            part.at[h, q, slot(h, 2, db), :, sub[way]], r1a.at[h, q, way, db],
            ss1a.at[h, q, way, db], rs1a.at[h, q, way, db], along(first_axis[h], step[way]))

    def send_1b(h, q, way, db, t):
        m1b[h, q, way, db, t] = launch(
            part.at[h, q, slot(h, step[way], db), :, sub[t]], r1b.at[h, q, way, db, :, sub[t]],
            ss1b.at[h, q, way, db, t], rs1b.at[h, q, way, db, t], along(first_axis[h], step[way]))

    def send_2a(h, q, way):
        m2a[h, q, way] = launch(
            part.at[h, q, slot(h, 0, 2), :, sub[way]], r2a.at[h, q, way],
            ss2a.at[h, q, way], rs2a.at[h, q, way], along(second_axis[h], step[way]))

    def send_2b(h, q, way, t):
        m2b[h, q, way, t] = launch(
            part.at[h, q, slot(h, 0, step[way]), :, sub[t]], r2b.at[h, q, way, :, sub[t]],
            ss2b.at[h, q, way, t], rs2b.at[h, q, way, t], along(second_axis[h], step[way]))

    def send_ready(q, i):
        todo = sorted(
            (WAVES.index(db), h, da, db)
            for h in range(2)
            for da, db in (p if h == 0 else p[::-1] for p in ORDER[SPLITS[q][i]:SPLITS[q][i + 1]])
        )
        for _, h, da, db in todo:
            if da == 2:
                for way in range(2):
                    send_1a(h, q, way, db)
        for _, h, da, db in todo:
            if da in (1, 3):
                way = step.index(da)
                send_1b(h, q, way, db, 1 - way)

    def normalise(q, i):
        for k in range(SPLITS[q][i], SPLITS[q][i + 1]):
            v = hid[q, k].astype(F32)
            hid[q, k] = (v * rms_scale(v) * gains[0]).astype(BF)

    def compute(q, i, between=lambda: None, following=None):
        k0, k1 = SPLITS[q][i], SPLITS[q][i + 1]
        rows = (k1 - k0) * tq
        if (q, i) == (0, 0):
            in_gains.wait()
            for k in range(k0, k1):
                hid_in[q, k].wait()
            normalise(q, i)
            in_wg.wait()
            in_wu.wait()
        if following:
            for k in range(SPLITS[following[0]][following[1]], SPLITS[following[0]][following[1] + 1]):
                hid_in[following[0], k].wait()
        v = hid[q, k0:k1].reshape(rows, d)
        gate = jnp.dot(v, wg[...], preferred_element_type=F32)
        up = jnp.dot(v, wu[...], preferred_element_type=F32)
        act[0:rows, :] = (gelu(gate) * up).astype(BF)
        if following:
            normalise(*following)
        between()
        if (q, i) == (0, 0):
            in_wd.wait()
        dt = min(DT, half)
        per = half // dt
        for j in range(2 * per):
            v = jnp.dot(act[0:rows, :], wd[:, j * dt:(j + 1) * dt], preferred_element_type=F32).astype(BF)
            part[j // per, q, k0:k1, :, (j % per) * dt:(j % per + 1) * dt] = v.reshape(k1 - k0, tq, dt)

    def add_into(h, q, k, t, other):
        part[h, q, k, :, sub[t]] = (part[h, q, k, :, sub[t]].astype(F32) + other[...].astype(F32)).astype(BF)

    def relay_1(q, db):
        for h in range(2):
            for way in range(2):
                m1a[h, q, way, db].wait_recv()
                add_into(h, q, slot(h, step[way], db), way, r1a.at[h, q, way, db])
                send_1b(h, q, way, db, way)

    def sum_1(q, db):
        for h in range(2):
            for way in range(2):
                for t in range(2):
                    m1b[h, q, way, db, t].wait_recv()
            k = slot(h, 0, db)
            total = part[h, q, k].astype(F32) + r1b[h, q, 0, db].astype(F32) + r1b[h, q, 1, db].astype(F32)
            part[h, q, k] = total.astype(BF)
            if db == 2:
                for way in range(2):
                    send_2a(h, q, way)
            elif db in (1, 3):
                way = step.index(db)
                send_2b(h, q, way, 1 - way)

    def relay_2(q):
        for h in range(2):
            for way in range(2):
                m2a[h, q, way].wait_recv()
                add_into(h, q, slot(h, 0, step[way]), way, r2a.at[h, q, way])
                send_2b(h, q, way, way)

    def serve():
        in_table.wait()
        rel = ids[...].reshape(ndev, tok) - ((g * SIDE * SIDE + m) * slab_rows).astype(F32)
        hit = (rel >= 0.0) & (rel < float(slab_rows))
        lane = lax.broadcasted_iota(jnp.int32, (ndev, tok), 1).astype(F32)
        first = jnp.min(jnp.where(hit, lane, 1e4), axis=1, keepdims=True)
        last = jnp.max(jnp.where(hit, lane, -1.0), axis=1, keepdims=True)
        id0 = jnp.sum(jnp.where(hit & (lane == first), rel, 0.0), axis=1, keepdims=True)
        id1 = jnp.sum(jnp.where(hit & (lane == last), rel, 0.0), axis=1, keepdims=True)
        id0 = jnp.where(first < 5e3, id0, -1.0).astype(jnp.int32)
        id1 = jnp.where(last > first, id1, -1.0).astype(jnp.int32)
        row_iota = lax.broadcasted_iota(jnp.int32, (ndev, slab_rows), 1)
        for i, wanted in enumerate((id0, id1)):
            pick = jnp.where(row_iota == wanted, 1.0, 0.0).astype(BF)
            served = jnp.dot(pick, table[...], preferred_element_type=F32)
            a0[:, :, :, :, :, i * pw:(i + 1) * pw] = served.reshape(nz, 2, SIDE, SIDE, 1, pw)

    def send_rows(stage):
        if stage == 0:
            a1[:, :, x, y] = a0[:, :, x, y]
            return exchange(
                members, lambda _, mm: a0.at[:, :, mm // SIDE, lax.rem(mm, SIDE)], a1.at[:, :, x, y], sx, rx, 0)
        a2[z, c] = a1[z, c]
        return exchange(groups, lambda gg, _: a1.at[gg // 2, lax.rem(gg, 2)], a2.at[z, c], sx, rx, nm)

    def look():
        target_col = diagonal_column(target_row, tok)
        i0 = lax.broadcasted_iota(jnp.int32, (tok, tok), 0)
        i1 = lax.broadcasted_iota(jnp.int32, (tok, tok), 1)
        second = jnp.max(jnp.where((target_col == target_row) & (i1 < i0), 1.0, 0.0), axis=1, keepdims=True)
        owners = lax.broadcasted_iota(jnp.int32, (tok, ndev), 1).astype(F32) == target_col
        rows = jnp.zeros((tok, pw), F32)
        for i in range(2):
            pick = jnp.where(owners & (second == float(i)), 1.0, 0.0).astype(BF)
            rows_i = a2[:, :, :, :, :, i * pw:(i + 1) * pw].reshape(ndev, pw).astype(BF)
            rows += jnp.dot(pick, rows_i, preferred_element_type=F32)
        looked[...] = rows * float(pw) ** 0.5

    nb = nz * 2
    channels = SIDE * SIDE * wb.shape[5]

    def finish(q):
        for h in range(2):
            for way in range(2):
                for t in range(2):
                    m2b[h, q, way, t].wait_recv()
        sums = [
            part[h, q, slot(h, 0, 0)].astype(F32) + r2b[h, q, 0].astype(F32) + r2b[h, q, 1].astype(F32)
            for h in range(2)
        ]
        mlp = jnp.concatenate(sums, axis=1)
        current = own[toks[q]].astype(F32) + mlp * rms_scale(mlp) * gains[1]
        current_b = current.astype(BF)
        gate = jnp.zeros((tq, channels), F32)
        for b in range(nb):
            w = wb[b // 2, b % 2, 0].reshape(channels, lanes)
            gate += lax.dot_general(
                current_b[:, b * lanes:(b + 1) * lanes], w, (((1,), (1,)), ((), ())), preferred_element_type=F32)
        ple_act = (gelu(gate) * looked[toks[q]]).astype(BF)
        ple = jnp.concatenate(
            [
                jnp.dot(ple_act, wb[b // 2, b % 2, 1].reshape(channels, lanes), preferred_element_type=F32)
                for b in range(nb)
            ],
            axis=1,
        )
        out[m, toks[q]] = (current + ple * rms_scale(ple) * gains[2]).astype(BF)

    g1, g2, g3, g4 = {}, {}, {}, {}

    def piece(h, q, da, db, t=None):
        lo = h * half + (0 if t is None else t * quarter)
        width = half if t is None else quarter
        return out.at[at(da, db) if h == 0 else at(db, da), toks[q], lo:lo + width]

    def publish(q):
        for h in range(2):
            for way in range(2):
                view = piece(h, q, 0, 0)
                g1[h, q, way] = launch(view, view, sg1.at[h, q, way], rg1.at[h, q, way],
                                       along(second_axis[h], step[way]))

    def spread(q, db):
        for h in range(2):
            for way in range(2):
                view = piece(h, q, 0, db)
                g3[h, q, way, db] = launch(view, view, sg3.at[h, q, way, db], rg3.at[h, q, way, db],
                                           along(first_axis[h], step[way]))

    def pass_on(q):
        for way in range(2):
            for h in range(2):
                g1[h, q, way].wait_recv()
                view = piece(h, q, 0, step[1 - way], way)
                g2[h, q, way] = launch(view, view, sg2.at[h, q, way], rg2.at[h, q, way],
                                       along(second_axis[h], step[way]))

    def settle(q):
        for h in range(2):
            for way in range(2):
                g2[h, q, way].wait_recv()

    def forward(q, db):
        for h in range(2):
            for way in range(2):
                g3[h, q, way, db].wait_recv()
                view = piece(h, q, step[1 - way], db, way)
                g4[h, q, way, db] = launch(view, view, sg4.at[h, q, way, db], rg4.at[h, q, way, db],
                                           along(first_axis[h], step[way]))

    fi = gather_ids(0)
    for copy in in_w:
        copy.wait()
    fw = gather_w(0)
    compute(0, 0, following=(0, 1))
    send_ready(0, 0)
    arrive(fi)
    fi = gather_ids(1)
    compute(0, 1, following=(0, 2))
    send_ready(0, 1)
    relay_1(0, 2)
    arrive(fi)
    serve()
    fx = send_rows(0)
    arrive(fw)
    fw = gather_w(1)
    compute(0, 2, following=(1, 0))
    send_ready(0, 2)
    relay_1(0, 1)
    relay_1(0, 3)
    relay_1(0, 0)
    compute(1, 0, following=(1, 1))
    sum_1(0, 2)
    send_ready(1, 0)
    arrive(fx)
    fx = send_rows(1)
    compute(1, 1)
    sum_1(0, 1)
    sum_1(0, 3)
    relay_2(0)
    send_ready(1, 1)
    arrive(fw)
    fw = gather_w(2)
    relay_1(1, 2)
    relay_1(1, 1)
    relay_1(1, 3)
    relay_1(1, 0)
    sum_1(0, 0)
    sum_1(1, 2)
    arrive(fx)
    in_own.wait()
    look()
    arrive(fw)
    finish(0)
    publish(0)
    spread(0, 0)
    sum_1(1, 1)
    sum_1(1, 3)
    relay_2(1)
    pass_on(0)
    spread(0, 1)
    spread(0, 3)
    sum_1(1, 0)
    settle(0)
    spread(0, 2)
    finish(1)
    publish(1)
    spread(1, 0)
    forward(0, 0)
    pass_on(1)
    spread(1, 1)
    spread(1, 3)
    forward(0, 1)
    forward(0, 3)
    settle(1)
    spread(1, 2)
    forward(0, 2)
    for db in (0, 1, 3, 2):
        forward(1, db)
    arrive(g4.values())
    for copy in started:
        copy.wait_send()


def per_device(
    hidden, token_slab, token_row, slab_owner, ple_table, norm_gains, w_gate, w_up, w_down, ple_gate, ple_proj
):
    members = lax.axis_size("member")
    nz = lax.axis_size("group") // 2
    tok = token_row.shape[0]
    d, n = w_gate.shape[1:]
    slab_rows, pw = ple_table.shape
    half, tq = d // 2, tok // 2
    per = ple_gate.shape[2]
    lanes = d // (2 * nz)
    dma = pltpu.SemaphoreType.DMA
    hbm, vmem = pl.BlockSpec(memory_space=pltpu.HBM), pl.BlockSpec(memory_space=pltpu.VMEM)
    stages = SIDE * SIDE + 2 * nz
    most = max(b - a for split in SPLITS for a, b in zip(split, split[1:]))
    rows_buf = pltpu.VMEM((nz, 2, SIDE, SIDE, 1, 2 * pw), F32)
    pairs = [
        (2, 2, 2, 4), (2, 2, 2, 4, 2), (2, 2, 2), (2, 2, 2, 2),
        (2, 2, 2), (2, 2, 2), (2, 2, 2, 4), (2, 2, 2, 4),
        (stages,), (stages,), (stages,),
    ]
    call = pl.pallas_call(
        functools.partial(body, nz, slab_rows),
        out_shape=jax.ShapeDtypeStruct((members, tok, d), BF),
        in_specs=[hbm] * 11,
        out_specs=vmem,
        scratch_shapes=[
            pltpu.VMEM((2, 16, tq, d), BF),
            pltpu.VMEM((tok, d), BF),
            pltpu.VMEM((d, n), BF),
            pltpu.VMEM((d, n), BF),
            pltpu.VMEM((n, d), BF),
            pltpu.VMEM((slab_rows, pw), BF),
            pltpu.VMEM((most * tq, n), BF),
            pltpu.VMEM((2, 2, 16, tq, half), BF),
            pltpu.VMEM((2, 2, 2, 4, tq, half // 2), BF),
            pltpu.VMEM((2, 2, 2, 4, tq, half), BF),
            pltpu.VMEM((2, 2, 2, tq, half // 2), BF),
            pltpu.VMEM((2, 2, 2, tq, half), BF),
            pltpu.VMEM((nz, 2, SIDE, SIDE, 1, tok), F32),
            rows_buf, rows_buf, rows_buf,
            pltpu.VMEM((nz, 2, 2, SIDE, SIDE, per, lanes), BF),
            pltpu.VMEM((3, 1, d), F32),
            pltpu.VMEM((1, tok), jnp.int32),
            pltpu.VMEM((1, tok), jnp.int32),
            pltpu.VMEM((1, slab_owner.shape[0]), jnp.int32),
            pltpu.VMEM((tok, pw), F32),
            dma((48,)),
        ] + [dma(shape) for shape in pairs for _ in range(2)],
        compiler_params=pltpu.CompilerParams(
            collective_id=0, has_side_effects=True, vmem_limit_bytes=40 * 1024 * 1024
        ),
        name="layer",
    )
    operands = (
        hidden.reshape(members, tok, d), w_gate[0], w_up[0], w_down[0], ple_gate[0].T, ple_proj[0], ple_table,
        norm_gains.reshape(3, 1, d), token_slab.reshape(1, tok), token_row.reshape(1, tok),
        slab_owner.reshape(1, -1),
    )
    out = call(*[pltpu.with_memory_space_constraint(v, pltpu.HBM) for v in operands])
    return out.reshape(members * tok, d)


def solution(mesh):
    return jax.shard_map(
        per_device,
        mesh=mesh,
        in_specs=(
            P("group", None),
            P(("group", "member"), None),
            P(("group", "member")),
            P(),
            P(("group", "member"), None),
            P(),
            P(None, None, "member"),
            P(None, None, "member"),
            P(None, "member", None),
            P(None, None, "member"),
            P(None, "member", None),
        ),
        out_specs=P("group", None),
        check_vma=False,
    )
```

```python
import functools

import jax
import jax.numpy as jnp
from jax import lax
from jax.experimental import pallas as pl
from jax.experimental.pallas import tpu as pltpu
from jax.sharding import PartitionSpec as P

EPS = 1e-06
MESH = pl.DeviceIdType.MESH
BF, F32 = jnp.bfloat16, jnp.float32
SIDE = 4
ORDER = [
    (2, 2), (1, 2), (2, 1), (3, 2), (2, 3),
    (1, 1), (1, 3), (3, 1), (3, 3), (0, 2), (2, 0),
    (0, 1), (1, 0), (0, 3), (3, 0), (0, 0),
]
SPLITS = ((0, 1, 5, 11, 16), (0, 8, 16))
DT = 1024
WAVES = (2, 1, 3, 0)


def slot(h, da, db):
    return ORDER.index((da, db) if h == 0 else (db, da))


def gelu(v):
    return 0.5 * v * (1.0 + jnp.tanh(0.7978845608028654 * (v + 0.044715 * (v * v * v))))


def rms_scale(v):
    return lax.rsqrt(jnp.mean(v * v, axis=-1, keepdims=True) + EPS)


def diagonal_column(row, n):
    eye = lax.broadcasted_iota(jnp.int32, (n, n), 0) == lax.broadcasted_iota(jnp.int32, (n, n), 1)
    return jnp.sum(jnp.where(eye, row, 0.0), axis=1, keepdims=True)


def body(
    nz, slab_rows,
    hid_hbm, wg_hbm, wu_hbm, wd_hbm, pg_hbm, pp_hbm, table_hbm, gains_hbm, slab_hbm, rowid_hbm, owner_hbm,
    out,
    hid, own, wg, wu, wd, table, act, part, r1a, r1b, r2a, r2b, ids, a0, a1, a2, wb,
    gains, slab, rowid, owner, looked,
    local_sem, ss1a, rs1a, ss1b, rs1b, ss2a, rs2a, ss2b, rs2b, sg1, rg1, sg2, rg2, sg3, rg3, sg4, rg4,
    sid, rid, sw, rw, sx, rx,
):
    tok, d = own.shape
    half, tq = d // 2, tok // 2
    quarter = half // 2
    lanes = wb.shape[-1]
    pw = table.shape[1]
    ndev = nz * 2 * SIDE * SIDE
    g, m = lax.axis_index("group"), lax.axis_index("member")
    z, c = g // 2, lax.rem(g, 2)
    x, y = m // SIDE, lax.rem(m, SIDE)
    toks = (slice(0, tq), slice(tq, tok))
    sub = (slice(0, quarter), slice(quarter, half))
    first_axis, second_axis = ("x", "y"), ("y", "x")
    step = (1, SIDE - 1)

    def at(dx, dy):
        return lax.rem(x + dx, SIDE) * SIDE + lax.rem(y + dy, SIDE)

    def along(axis, off):
        if axis == "x":
            return (g, at(off, 0))
        if axis == "y":
            return (g, at(0, off))
        if axis == "z":
            return (lax.rem(z + off, nz) * 2 + c, m)
        return (z * 2 + 1 - c, m)

    shifts = [(dx, dy) for dx in range(SIDE) for dy in range(SIDE) if dx or dy]
    members = [(g, at(dx, dy)) for dx, dy in shifts]
    groups = [(lax.rem(g + o, 2 * nz), m) for o in range(1, 2 * nz)]
    peers = members + groups

    barrier = pltpu.get_barrier_semaphore()
    for peer in peers:
        pl.semaphore_signal(barrier, inc=1, device_id=peer, device_id_type=MESH)

    locals_ = []

    def local(src, dst):
        copy = pltpu.make_async_copy(src, dst, local_sem.at[len(locals_)])
        copy.start()
        locals_.append(copy)
        return copy

    in_small = [local(owner_hbm, owner), local(slab_hbm, slab), local(rowid_hbm, rowid)]
    in_gains = local(gains_hbm, gains)
    hid_in = {}

    def load_hidden(q, k0, k1):
        for k in range(k0, k1):
            hid_in[q, k] = local(hid_hbm.at[at(*ORDER[k]), toks[q]], hid.at[q, k])

    load_hidden(0, 0, 1)
    lane0 = pl.multiple_of(g * lanes, 128)
    in_w = [
        local(pg_hbm.at[:, pl.ds(lane0, lanes)], wb.at[z, c, 0, x, y]),
        local(pp_hbm.at[:, pl.ds(lane0, lanes)], wb.at[z, c, 1, x, y]),
    ]
    in_wg = local(wg_hbm, wg)
    in_wu = local(wu_hbm, wu)
    in_wd = local(wd_hbm, wd)
    load_hidden(0, 1, 16)
    load_hidden(1, 0, 16)
    in_table = local(table_hbm, table)
    in_own = local(hid_hbm.at[m], own)

    for copy in in_small:
        copy.wait()
    owner_col = diagonal_column(owner[...].astype(F32), ndev)
    match = lax.broadcasted_iota(jnp.int32, (ndev, tok), 0) == slab[...]
    target_row = jnp.sum(jnp.where(match, owner_col, 0.0), axis=0, keepdims=True)
    ids[z, c, x, y] = target_row * float(slab_rows) + rowid[...].astype(F32)

    pl.semaphore_wait(barrier, len(peers))

    started = []

    def launch(src, dst, s, r, dev):
        copy = pltpu.make_async_remote_copy(
            src_ref=src, dst_ref=dst, send_sem=s, recv_sem=r, device_id=dev, device_id_type=MESH
        )
        copy.start()
        started.append(copy)
        return copy

    drained = []

    def drain(upto):
        for copy in started[len(drained):upto]:
            copy.wait_send()
            drained.append(copy)

    def exchange(devices, ref_of, dst, s, r, base):
        return [
            launch(ref_of(*device), dst, s.at[base + i], r.at[base + i], device) for i, device in enumerate(devices)
        ]

    def arrive(copies):
        for copy in copies:
            copy.wait_recv()

    nm, ng = len(members), len(groups)

    def same(devices, view, s, r, base):
        return exchange(devices, lambda *_: view, view, s, r, base)

    def gather_ids(stage):
        if stage == 0:
            return same(members, ids.at[z, c, x, y], sid, rid, 0)
        return same(groups, ids.at[z, c], sid, rid, nm)

    def gather_w(stage):
        if stage == 0:
            return same(members, wb.at[z, c, :, x, y], sw, rw, 0)
        if stage == 1:
            return same([along("z", o) for o in range(1, nz)], wb.at[z, c], sw, rw, nm)
        return same([along("c", 1)], wb.at[:, c], sw, rw, nm + nz - 1)

    m1a, m1b, m2a, m2b = {}, {}, {}, {}

    def send_1a(h, q, way, db):
        m1a[h, q, way, db] = launch(
            part.at[h, q, slot(h, 2, db), :, sub[way]], r1a.at[h, q, way, db],
            ss1a.at[h, q, way, db], rs1a.at[h, q, way, db], along(first_axis[h], step[way]))

    def send_1b(h, q, way, db, t):
        m1b[h, q, way, db, t] = launch(
            part.at[h, q, slot(h, step[way], db), :, sub[t]], r1b.at[h, q, way, db, :, sub[t]],
            ss1b.at[h, q, way, db, t], rs1b.at[h, q, way, db, t], along(first_axis[h], step[way]))

    def send_2a(h, q, way):
        m2a[h, q, way] = launch(
            part.at[h, q, slot(h, 0, 2), :, sub[way]], r2a.at[h, q, way],
            ss2a.at[h, q, way], rs2a.at[h, q, way], along(second_axis[h], step[way]))

    def send_2b(h, q, way, t):
        m2b[h, q, way, t] = launch(
            part.at[h, q, slot(h, 0, step[way]), :, sub[t]], r2b.at[h, q, way, :, sub[t]],
            ss2b.at[h, q, way, t], rs2b.at[h, q, way, t], along(second_axis[h], step[way]))

    def send_ready(q, i):
        todo = sorted(
            (WAVES.index(db), h, da, db)
            for h in range(2)
            for da, db in (p if h == 0 else p[::-1] for p in ORDER[SPLITS[q][i]:SPLITS[q][i + 1]])
        )
        for _, h, da, db in todo:
            if da == 2:
                for way in range(2):
                    send_1a(h, q, way, db)
        for _, h, da, db in todo:
            if da in (1, 3):
                way = step.index(da)
                send_1b(h, q, way, db, 1 - way)

    def normalise(q, i):
        for k in range(SPLITS[q][i], SPLITS[q][i + 1]):
            v = hid[q, k].astype(F32)
            hid[q, k] = (v * rms_scale(v) * gains[0]).astype(BF)

    def compute(q, i, between=lambda: None, following=None):
        k0, k1 = SPLITS[q][i], SPLITS[q][i + 1]
        rows = (k1 - k0) * tq
        if (q, i) == (0, 0):
            in_gains.wait()
            for k in range(k0, k1):
                hid_in[q, k].wait()
            normalise(q, i)
            in_wg.wait()
            in_wu.wait()
        if following:
            for k in range(SPLITS[following[0]][following[1]], SPLITS[following[0]][following[1] + 1]):
                hid_in[following[0], k].wait()
        v = hid[q, k0:k1].reshape(rows, d)
        gate = jnp.dot(v, wg[...], preferred_element_type=F32)
        up = jnp.dot(v, wu[...], preferred_element_type=F32)
        act[0:rows, :] = (gelu(gate) * up).astype(BF)
        if following:
            normalise(*following)
        between()
        if (q, i) == (0, 0):
            in_wd.wait()
        dt = min(DT, half)
        per = half // dt
        for j in range(2 * per):
            v = jnp.dot(act[0:rows, :], wd[:, j * dt:(j + 1) * dt], preferred_element_type=F32).astype(BF)
            part[j // per, q, k0:k1, :, (j % per) * dt:(j % per + 1) * dt] = v.reshape(k1 - k0, tq, dt)

    def add_into(h, q, k, t, other):
        part[h, q, k, :, sub[t]] = (part[h, q, k, :, sub[t]].astype(F32) + other[...].astype(F32)).astype(BF)

    def relay_1(q, db):
        for h in range(2):
            for way in range(2):
                m1a[h, q, way, db].wait_recv()
                add_into(h, q, slot(h, step[way], db), way, r1a.at[h, q, way, db])
                send_1b(h, q, way, db, way)

    def sum_1(q, db):
        for h in range(2):
            for way in range(2):
                for t in range(2):
                    m1b[h, q, way, db, t].wait_recv()
            k = slot(h, 0, db)
            total = part[h, q, k].astype(F32) + r1b[h, q, 0, db].astype(F32) + r1b[h, q, 1, db].astype(F32)
            part[h, q, k] = total.astype(BF)
            if db == 2:
                for way in range(2):
                    send_2a(h, q, way)
            elif db in (1, 3):
                way = step.index(db)
                send_2b(h, q, way, 1 - way)

    def relay_2(q):
        for h in range(2):
            for way in range(2):
                m2a[h, q, way].wait_recv()
                add_into(h, q, slot(h, 0, step[way]), way, r2a.at[h, q, way])
                send_2b(h, q, way, way)

    def serve():
        in_table.wait()
        rel = ids[...].reshape(ndev, tok) - ((g * SIDE * SIDE + m) * slab_rows).astype(F32)
        hit = (rel >= 0.0) & (rel < float(slab_rows))
        lane = lax.broadcasted_iota(jnp.int32, (ndev, tok), 1).astype(F32)
        first = jnp.min(jnp.where(hit, lane, 1e4), axis=1, keepdims=True)
        last = jnp.max(jnp.where(hit, lane, -1.0), axis=1, keepdims=True)
        id0 = jnp.sum(jnp.where(hit & (lane == first), rel, 0.0), axis=1, keepdims=True)
        id1 = jnp.sum(jnp.where(hit & (lane == last), rel, 0.0), axis=1, keepdims=True)
        id0 = jnp.where(first < 5e3, id0, -1.0).astype(jnp.int32)
        id1 = jnp.where(last > first, id1, -1.0).astype(jnp.int32)
        row_iota = lax.broadcasted_iota(jnp.int32, (ndev, slab_rows), 1)
        for i, wanted in enumerate((id0, id1)):
            pick = jnp.where(row_iota == wanted, 1.0, 0.0).astype(BF)
            served = jnp.dot(pick, table[...], preferred_element_type=F32)
            a0[:, :, :, :, i, :] = served.astype(BF).reshape(nz, 2, SIDE, SIDE, pw)

    def send_rows(stage):
        if stage == 0:
            a1[:, :, x, y] = a0[:, :, x, y]
            return exchange(
                members, lambda _, mm: a0.at[:, :, mm // SIDE, lax.rem(mm, SIDE)], a1.at[:, :, x, y], sx, rx, 0)
        a2[z, c] = a1[z, c]
        return exchange(groups, lambda gg, _: a1.at[gg // 2, lax.rem(gg, 2)], a2.at[z, c], sx, rx, nm)

    def look():
        target_col = diagonal_column(target_row, tok)
        i0 = lax.broadcasted_iota(jnp.int32, (tok, tok), 0)
        i1 = lax.broadcasted_iota(jnp.int32, (tok, tok), 1)
        second = jnp.max(jnp.where((target_col == target_row) & (i1 < i0), 1.0, 0.0), axis=1, keepdims=True)
        owners = lax.broadcasted_iota(jnp.int32, (tok, ndev), 1).astype(F32) == target_col
        rows = jnp.zeros((tok, pw), F32)
        for i in range(2):
            pick = jnp.where(owners & (second == float(i)), 1.0, 0.0).astype(BF)
            rows_i = a2[:, :, :, :, i, :].reshape(ndev, pw)
            rows += jnp.dot(pick, rows_i, preferred_element_type=F32)
        looked[...] = rows * float(pw) ** 0.5

    nb = nz * 2
    channels = SIDE * SIDE * wb.shape[5]

    def finish(q):
        for h in range(2):
            for way in range(2):
                for t in range(2):
                    m2b[h, q, way, t].wait_recv()
        sums = [
            part[h, q, slot(h, 0, 0)].astype(F32) + r2b[h, q, 0].astype(F32) + r2b[h, q, 1].astype(F32)
            for h in range(2)
        ]
        mlp = jnp.concatenate(sums, axis=1)
        current = own[toks[q]].astype(F32) + mlp * rms_scale(mlp) * gains[1]
        current_b = current.astype(BF)
        gate = jnp.zeros((tq, channels), F32)
        for b in range(nb):
            w = wb[b // 2, b % 2, 0].reshape(channels, lanes)
            gate += lax.dot_general(
                current_b[:, b * lanes:(b + 1) * lanes], w, (((1,), (1,)), ((), ())), preferred_element_type=F32)
        ple_act = (gelu(gate) * looked[toks[q]]).astype(BF)
        ple = jnp.concatenate(
            [
                jnp.dot(ple_act, wb[b // 2, b % 2, 1].reshape(channels, lanes), preferred_element_type=F32)
                for b in range(nb)
            ],
            axis=1,
        )
        out[m, toks[q]] = (current + ple * rms_scale(ple) * gains[2]).astype(BF)

    g1, g2, g3, g4 = {}, {}, {}, {}

    def piece(h, q, da, db, t=None):
        lo = h * half + (0 if t is None else t * quarter)
        width = half if t is None else quarter
        return out.at[at(da, db) if h == 0 else at(db, da), toks[q], lo:lo + width]

    def publish(q):
        for h in range(2):
            for way in range(2):
                view = piece(h, q, 0, 0)
                g1[h, q, way] = launch(view, view, sg1.at[h, q, way], rg1.at[h, q, way],
                                       along(second_axis[h], step[way]))

    def spread(q, db):
        for h in range(2):
            for way in range(2):
                view = piece(h, q, 0, db)
                g3[h, q, way, db] = launch(view, view, sg3.at[h, q, way, db], rg3.at[h, q, way, db],
                                           along(first_axis[h], step[way]))

    def pass_on(q):
        for way in range(2):
            for h in range(2):
                g1[h, q, way].wait_recv()
                view = piece(h, q, 0, step[1 - way], way)
                g2[h, q, way] = launch(view, view, sg2.at[h, q, way], rg2.at[h, q, way],
                                       along(second_axis[h], step[way]))

    def settle(q):
        for h in range(2):
            for way in range(2):
                g2[h, q, way].wait_recv()

    def forward(q, db):
        for h in range(2):
            for way in range(2):
                g3[h, q, way, db].wait_recv()
                view = piece(h, q, step[1 - way], db, way)
                g4[h, q, way, db] = launch(view, view, sg4.at[h, q, way, db], rg4.at[h, q, way, db],
                                           along(first_axis[h], step[way]))

    fi = gather_ids(0)
    for copy in in_w:
        copy.wait()
    fw = gather_w(0)
    compute(0, 0)
    send_ready(0, 0)
    for k in range(SPLITS[0][1], SPLITS[0][2]):
        hid_in[0, k].wait()
    normalise(0, 1)
    compute(0, 1, following=(0, 2))
    send_ready(0, 1)
    arrive(fi)
    fi = gather_ids(1)
    compute(0, 2, following=(0, 3))
    send_ready(0, 2)
    relay_1(0, 2)
    arrive(fi)
    serve()
    fx = send_rows(0)
    arrive(fw)
    fw = gather_w(1)
    compute(0, 3, following=(1, 0))
    send_ready(0, 3)
    relay_1(0, 1)
    relay_1(0, 3)
    relay_1(0, 0)
    compute(1, 0, following=(1, 1))
    sum_1(0, 2)
    send_ready(1, 0)
    arrive(fx)
    fx = send_rows(1)
    compute(1, 1)
    sum_1(0, 1)
    sum_1(0, 3)
    relay_2(0)
    send_ready(1, 1)
    arrive(fw)
    fw = gather_w(2)
    relay_1(1, 2)
    relay_1(1, 1)
    relay_1(1, 3)
    relay_1(1, 0)
    sum_1(0, 0)
    sum_1(1, 2)
    arrive(fx)
    in_own.wait()
    look()
    arrive(fw)
    finish(0)
    n0 = len(started)
    publish(0)
    spread(0, 0)
    sum_1(1, 1)
    sum_1(1, 3)
    relay_2(1)
    pass_on(0)
    spread(0, 1)
    spread(0, 3)
    sum_1(1, 0)
    settle(0)
    spread(0, 2)
    finish(1)
    n1 = len(started)
    publish(1)
    spread(1, 0)
    drain(n0)
    forward(0, 0)
    pass_on(1)
    spread(1, 1)
    spread(1, 3)
    forward(0, 1)
    forward(0, 3)
    settle(1)
    spread(1, 2)
    forward(0, 2)
    n2 = len(started)
    forward(1, 0)
    drain(n1)
    for db in (1, 3, 2):
        forward(1, db)
    drain(n2)
    arrive(g4.values())
    drain(len(started))


def per_device(
    hidden, token_slab, token_row, slab_owner, ple_table, norm_gains, w_gate, w_up, w_down, ple_gate, ple_proj
):
    members = lax.axis_size("member")
    nz = lax.axis_size("group") // 2
    tok = token_row.shape[0]
    d, n = w_gate.shape[1:]
    slab_rows, pw = ple_table.shape
    half, tq = d // 2, tok // 2
    per = ple_gate.shape[2]
    lanes = d // (2 * nz)
    dma = pltpu.SemaphoreType.DMA
    hbm, vmem = pl.BlockSpec(memory_space=pltpu.HBM), pl.BlockSpec(memory_space=pltpu.VMEM)
    stages = SIDE * SIDE + 2 * nz
    most = max(b - a for split in SPLITS for a, b in zip(split, split[1:]))
    rows_buf = pltpu.VMEM((nz, 2, SIDE, SIDE, 2, pw), BF)
    pairs = [
        (2, 2, 2, 4), (2, 2, 2, 4, 2), (2, 2, 2), (2, 2, 2, 2),
        (2, 2, 2), (2, 2, 2), (2, 2, 2, 4), (2, 2, 2, 4),
        (stages,), (stages,), (stages,),
    ]
    call = pl.pallas_call(
        functools.partial(body, nz, slab_rows),
        out_shape=jax.ShapeDtypeStruct((members, tok, d), BF),
        in_specs=[hbm] * 11,
        out_specs=vmem,
        scratch_shapes=[
            pltpu.VMEM((2, 16, tq, d), BF),
            pltpu.VMEM((tok, d), BF),
            pltpu.VMEM((d, n), BF),
            pltpu.VMEM((d, n), BF),
            pltpu.VMEM((n, d), BF),
            pltpu.VMEM((slab_rows, pw), BF),
            pltpu.VMEM((most * tq, n), BF),
            pltpu.VMEM((2, 2, 16, tq, half), BF),
            pltpu.VMEM((2, 2, 2, 4, tq, half // 2), BF),
            pltpu.VMEM((2, 2, 2, 4, tq, half), BF),
            pltpu.VMEM((2, 2, 2, tq, half // 2), BF),
            pltpu.VMEM((2, 2, 2, tq, half), BF),
            pltpu.VMEM((nz, 2, SIDE, SIDE, 1, tok), F32),
            rows_buf, rows_buf, rows_buf,
            pltpu.VMEM((nz, 2, 2, SIDE, SIDE, per, lanes), BF),
            pltpu.VMEM((3, 1, d), F32),
            pltpu.VMEM((1, tok), jnp.int32),
            pltpu.VMEM((1, tok), jnp.int32),
            pltpu.VMEM((1, slab_owner.shape[0]), jnp.int32),
            pltpu.VMEM((tok, pw), F32),
            dma((48,)),
        ] + [dma(shape) for shape in pairs for _ in range(2)],
        compiler_params=pltpu.CompilerParams(
            collective_id=0, has_side_effects=True, vmem_limit_bytes=40 * 1024 * 1024
        ),
        name="layer",
    )
    operands = (
        hidden.reshape(members, tok, d), w_gate[0], w_up[0], w_down[0], ple_gate[0].T, ple_proj[0], ple_table,
        norm_gains.reshape(3, 1, d), token_slab.reshape(1, tok), token_row.reshape(1, tok),
        slab_owner.reshape(1, -1),
    )
    out = call(*[pltpu.with_memory_space_constraint(v, pltpu.HBM) for v in operands])
    return out.reshape(members * tok, d)


def solution(mesh):
    return jax.shard_map(
        per_device,
        mesh=mesh,
        in_specs=(
            P("group", None),
            P(("group", "member"), None),
            P(("group", "member")),
            P(),
            P(("group", "member"), None),
            P(),
            P(None, None, "member"),
            P(None, None, "member"),
            P(None, "member", None),
            P(None, None, "member"),
            P(None, "member", None),
        ),
        out_specs=P("group", None),
        check_vma=False,
    )
```

```python
import functools

import jax
import jax.numpy as jnp
from jax import lax
from jax.experimental import pallas as pl
from jax.experimental.pallas import tpu as pltpu
from jax.sharding import PartitionSpec as P

EPS = 1e-06
MESH = pl.DeviceIdType.MESH
BF, F32 = jnp.bfloat16, jnp.float32
SIDE = 4
ORDER = [
    (2, 2), (1, 2), (2, 1), (3, 2), (2, 3),
    (1, 1), (1, 3), (3, 1), (3, 3), (0, 2), (2, 0),
    (0, 1), (1, 0), (0, 3), (3, 0), (0, 0),
]
SPLITS = ((0, 1, 5, 11, 16), (0, 8, 16))
DT = 1024
WAVES = (2, 1, 3, 0)


def slot(h, da, db):
    return ORDER.index((da, db) if h == 0 else (db, da))


def gelu(v):
    return 0.5 * v * (1.0 + jnp.tanh(0.7978845608028654 * (v + 0.044715 * (v * v * v))))


def rms_scale(v):
    return lax.rsqrt(jnp.mean(v * v, axis=-1, keepdims=True) + EPS)


def diagonal_column(row, n):
    eye = lax.broadcasted_iota(jnp.int32, (n, n), 0) == lax.broadcasted_iota(jnp.int32, (n, n), 1)
    return jnp.sum(jnp.where(eye, row, 0.0), axis=1, keepdims=True)


def body(
    nz, slab_rows,
    hid_hbm, wg_hbm, wu_hbm, wd_hbm, pg_hbm, pp_hbm, table_hbm, gains_hbm, slab_hbm, rowid_hbm, owner_hbm,
    out,
    hid, own, wg, wu, wd, table, act, part, r1a, r1b, r2a, r2b, ids, a0, a1, a2, wb,
    gains, slab, rowid, owner, looked,
    local_sem, ss1a, rs1a, ss1b, rs1b, ss2a, rs2a, ss2b, rs2b, sg1, rg1, sg2, rg2, sg3, rg3, sg4, rg4,
    sid, rid, sw, rw, sx, rx,
):
    tok, d = own.shape
    half, tq = d // 2, tok // 2
    quarter = half // 2
    lanes = wb.shape[-1]
    pw = table.shape[1]
    ndev = nz * 2 * SIDE * SIDE
    g, m = lax.axis_index("group"), lax.axis_index("member")
    z, c = g // 2, lax.rem(g, 2)
    x, y = m // SIDE, lax.rem(m, SIDE)
    toks = (slice(0, tq), slice(tq, tok))
    sub = (slice(0, quarter), slice(quarter, half))
    first_axis, second_axis = ("x", "y"), ("y", "x")
    step = (1, SIDE - 1)

    def at(dx, dy):
        return lax.rem(x + dx, SIDE) * SIDE + lax.rem(y + dy, SIDE)

    def along(axis, off):
        if axis == "x":
            return (g, at(off, 0))
        if axis == "y":
            return (g, at(0, off))
        if axis == "z":
            return (lax.rem(z + off, nz) * 2 + c, m)
        return (z * 2 + 1 - c, m)

    shifts = [(dx, dy) for dx in range(SIDE) for dy in range(SIDE) if dx or dy]
    members = [(g, at(dx, dy)) for dx, dy in shifts]
    groups = [(lax.rem(g + o, 2 * nz), m) for o in range(1, 2 * nz)]
    peers = members + groups

    barrier = pltpu.get_barrier_semaphore()
    for peer in peers:
        pl.semaphore_signal(barrier, inc=1, device_id=peer, device_id_type=MESH)

    locals_ = []

    def local(src, dst):
        copy = pltpu.make_async_copy(src, dst, local_sem.at[len(locals_)])
        copy.start()
        locals_.append(copy)
        return copy

    in_small = [local(owner_hbm, owner), local(slab_hbm, slab), local(rowid_hbm, rowid)]
    in_gains = local(gains_hbm, gains)
    hid_in = {}

    def load_hidden(q, k0, k1):
        for k in range(k0, k1):
            hid_in[q, k] = local(hid_hbm.at[at(*ORDER[k]), toks[q]], hid.at[q, k])

    load_hidden(0, 0, 1)
    lane0 = pl.multiple_of(g * lanes, 128)
    in_w = [
        local(pg_hbm.at[:, pl.ds(lane0, lanes)], wb.at[z, c, 0, x, y]),
        local(pp_hbm.at[:, pl.ds(lane0, lanes)], wb.at[z, c, 1, x, y]),
    ]
    in_wg = local(wg_hbm, wg)
    in_wu = local(wu_hbm, wu)
    in_wd = local(wd_hbm, wd)
    load_hidden(0, 1, 16)
    load_hidden(1, 0, 16)
    in_table = local(table_hbm, table)
    in_own = local(hid_hbm.at[m], own)

    for copy in in_small:
        copy.wait()
    owner_col = diagonal_column(owner[...].astype(F32), ndev)
    match = lax.broadcasted_iota(jnp.int32, (ndev, tok), 0) == slab[...]
    target_row = jnp.sum(jnp.where(match, owner_col, 0.0), axis=0, keepdims=True)
    ids[z, c, x, y] = target_row * float(slab_rows) + rowid[...].astype(F32)

    pl.semaphore_wait(barrier, len(peers))

    started = []

    def launch(src, dst, s, r, dev):
        copy = pltpu.make_async_remote_copy(
            src_ref=src, dst_ref=dst, send_sem=s, recv_sem=r, device_id=dev, device_id_type=MESH
        )
        copy.start()
        started.append(copy)
        return copy

    drained = []

    def drain(upto):
        for copy in started[len(drained):upto]:
            copy.wait_send()
            drained.append(copy)

    def exchange(devices, ref_of, dst, s, r, base):
        return [
            launch(ref_of(*device), dst, s.at[base + i], r.at[base + i], device) for i, device in enumerate(devices)
        ]

    def arrive(copies):
        for copy in copies:
            copy.wait_recv()

    nm, ng = len(members), len(groups)

    def same(devices, view, s, r, base):
        return exchange(devices, lambda *_: view, view, s, r, base)

    def gather_ids(stage):
        if stage == 0:
            return same(members, ids.at[z, c, x, y], sid, rid, 0)
        return same(groups, ids.at[z, c], sid, rid, nm)

    def gather_w(stage):
        if stage == 0:
            return same(members, wb.at[z, c, :, x, y], sw, rw, 0)
        if stage == 1:
            return same([along("z", o) for o in range(1, nz)], wb.at[z, c], sw, rw, nm)
        return same([along("c", 1)], wb.at[:, c], sw, rw, nm + nz - 1)

    m1a, m1b, m2a, m2b = {}, {}, {}, {}

    def send_1a(h, q, way, db):
        m1a[h, q, way, db] = launch(
            part.at[h, q, slot(h, 2, db), :, sub[way]], r1a.at[h, q, way, db],
            ss1a.at[h, q, way, db], rs1a.at[h, q, way, db], along(first_axis[h], step[way]))

    def send_1b(h, q, way, db, t):
        m1b[h, q, way, db, t] = launch(
            part.at[h, q, slot(h, step[way], db), :, sub[t]], r1b.at[h, q, way, db, :, sub[t]],
            ss1b.at[h, q, way, db, t], rs1b.at[h, q, way, db, t], along(first_axis[h], step[way]))

    def send_2a(h, q, way):
        m2a[h, q, way] = launch(
            part.at[h, q, slot(h, 0, 2), :, sub[way]], r2a.at[h, q, way],
            ss2a.at[h, q, way], rs2a.at[h, q, way], along(second_axis[h], step[way]))

    def send_2b(h, q, way, t):
        m2b[h, q, way, t] = launch(
            part.at[h, q, slot(h, 0, step[way]), :, sub[t]], r2b.at[h, q, way, :, sub[t]],
            ss2b.at[h, q, way, t], rs2b.at[h, q, way, t], along(second_axis[h], step[way]))

    def send_ready(q, i):
        todo = sorted(
            (WAVES.index(db), h, da, db)
            for h in range(2)
            for da, db in (p if h == 0 else p[::-1] for p in ORDER[SPLITS[q][i]:SPLITS[q][i + 1]])
        )
        for _, h, da, db in todo:
            if da == 2:
                for way in range(2):
                    send_1a(h, q, way, db)
        for _, h, da, db in todo:
            if da in (1, 3):
                way = step.index(da)
                send_1b(h, q, way, db, 1 - way)

    def normalise(q, i):
        for k in range(SPLITS[q][i], SPLITS[q][i + 1]):
            v = hid[q, k].astype(F32)
            hid[q, k] = (v * rms_scale(v) * gains[0]).astype(BF)

    def compute(q, i, between=lambda: None, following=None):
        k0, k1 = SPLITS[q][i], SPLITS[q][i + 1]
        rows = (k1 - k0) * tq
        if (q, i) == (0, 0):
            in_gains.wait()
            for k in range(k0, k1):
                hid_in[q, k].wait()
            normalise(q, i)
            in_wg.wait()
            in_wu.wait()
        if following:
            for k in range(SPLITS[following[0]][following[1]], SPLITS[following[0]][following[1] + 1]):
                hid_in[following[0], k].wait()
        v = hid[q, k0:k1].reshape(rows, d)
        gate = jnp.dot(v, wg[...], preferred_element_type=F32)
        up = jnp.dot(v, wu[...], preferred_element_type=F32)
        act[0:rows, :] = (gelu(gate) * up).astype(BF)
        if following:
            normalise(*following)
        between()
        if (q, i) == (0, 0):
            in_wd.wait()
        dt = min(DT, half)
        per = half // dt
        for j in range(2 * per):
            v = jnp.dot(act[0:rows, :], wd[:, j * dt:(j + 1) * dt], preferred_element_type=F32).astype(BF)
            part[j // per, q, k0:k1, :, (j % per) * dt:(j % per + 1) * dt] = v.reshape(k1 - k0, tq, dt)

    def add_into(h, q, k, t, other):
        part[h, q, k, :, sub[t]] = (part[h, q, k, :, sub[t]].astype(F32) + other[...].astype(F32)).astype(BF)

    def relay_1(q, db):
        for h in range(2):
            for way in range(2):
                m1a[h, q, way, db].wait_recv()
                add_into(h, q, slot(h, step[way], db), way, r1a.at[h, q, way, db])
                send_1b(h, q, way, db, way)

    def sum_1(q, db):
        for h in range(2):
            for way in range(2):
                for t in range(2):
                    m1b[h, q, way, db, t].wait_recv()
            k = slot(h, 0, db)
            total = part[h, q, k].astype(F32) + r1b[h, q, 0, db].astype(F32) + r1b[h, q, 1, db].astype(F32)
            part[h, q, k] = total.astype(BF)
            if db == 2:
                for way in range(2):
                    send_2a(h, q, way)
            elif db in (1, 3):
                way = step.index(db)
                send_2b(h, q, way, 1 - way)

    def relay_2(q):
        for h in range(2):
            for way in range(2):
                m2a[h, q, way].wait_recv()
                add_into(h, q, slot(h, 0, step[way]), way, r2a.at[h, q, way])
                send_2b(h, q, way, way)

    def serve():
        in_table.wait()
        rel = ids[...].reshape(ndev, tok) - ((g * SIDE * SIDE + m) * slab_rows).astype(F32)
        hit = (rel >= 0.0) & (rel < float(slab_rows))
        lane = lax.broadcasted_iota(jnp.int32, (ndev, tok), 1).astype(F32)
        first = jnp.min(jnp.where(hit, lane, 1e4), axis=1, keepdims=True)
        last = jnp.max(jnp.where(hit, lane, -1.0), axis=1, keepdims=True)
        id0 = jnp.sum(jnp.where(hit & (lane == first), rel, 0.0), axis=1, keepdims=True)
        id1 = jnp.sum(jnp.where(hit & (lane == last), rel, 0.0), axis=1, keepdims=True)
        id0 = jnp.where(first < 5e3, id0, -1.0).astype(jnp.int32)
        id1 = jnp.where(last > first, id1, -1.0).astype(jnp.int32)
        row_iota = lax.broadcasted_iota(jnp.int32, (ndev, slab_rows), 1)
        for i, wanted in enumerate((id0, id1)):
            pick = jnp.where(row_iota == wanted, 1.0, 0.0).astype(BF)
            served = jnp.dot(pick, table[...], preferred_element_type=F32)
            a0[:, :, :, :, i, :] = served.astype(BF).reshape(nz, 2, SIDE, SIDE, pw)

    def send_rows(stage):
        if stage == 0:
            a1[:, :, x, y] = a0[:, :, x, y]
            return exchange(
                members, lambda _, mm: a0.at[:, :, mm // SIDE, lax.rem(mm, SIDE)], a1.at[:, :, x, y], sx, rx, 0)
        a2[z, c] = a1[z, c]
        return exchange(groups, lambda gg, _: a1.at[gg // 2, lax.rem(gg, 2)], a2.at[z, c], sx, rx, nm)

    def look():
        target_col = diagonal_column(target_row, tok)
        i0 = lax.broadcasted_iota(jnp.int32, (tok, tok), 0)
        i1 = lax.broadcasted_iota(jnp.int32, (tok, tok), 1)
        second = jnp.max(jnp.where((target_col == target_row) & (i1 < i0), 1.0, 0.0), axis=1, keepdims=True)
        owners = lax.broadcasted_iota(jnp.int32, (tok, ndev), 1).astype(F32) == target_col
        rows = jnp.zeros((tok, pw), F32)
        for i in range(2):
            pick = jnp.where(owners & (second == float(i)), 1.0, 0.0).astype(BF)
            rows_i = a2[:, :, :, :, i, :].reshape(ndev, pw)
            rows += jnp.dot(pick, rows_i, preferred_element_type=F32)
        looked[...] = rows * float(pw) ** 0.5

    nb = nz * 2
    channels = SIDE * SIDE * wb.shape[5]

    def finish(q):
        for h in range(2):
            for way in range(2):
                for t in range(2):
                    m2b[h, q, way, t].wait_recv()
        sums = [
            part[h, q, slot(h, 0, 0)].astype(F32) + r2b[h, q, 0].astype(F32) + r2b[h, q, 1].astype(F32)
            for h in range(2)
        ]
        mlp = jnp.concatenate(sums, axis=1)
        current = own[toks[q]].astype(F32) + mlp * rms_scale(mlp) * gains[1]
        current_b = current.astype(BF)
        gate = jnp.zeros((tq, channels), F32)
        for b in range(nb):
            w = wb[b // 2, b % 2, 0].reshape(channels, lanes)
            gate += lax.dot_general(
                current_b[:, b * lanes:(b + 1) * lanes], w, (((1,), (1,)), ((), ())), preferred_element_type=F32)
        ple_act = (gelu(gate) * looked[toks[q]]).astype(BF)
        ple = jnp.concatenate(
            [
                jnp.dot(ple_act, wb[b // 2, b % 2, 1].reshape(channels, lanes), preferred_element_type=F32)
                for b in range(nb)
            ],
            axis=1,
        )
        out[m, toks[q]] = (current + ple * rms_scale(ple) * gains[2]).astype(BF)

    g1, g2, g3, g4 = {}, {}, {}, {}

    def piece(h, q, da, db, t=None):
        lo = h * half + (0 if t is None else t * quarter)
        width = half if t is None else quarter
        return out.at[at(da, db) if h == 0 else at(db, da), toks[q], lo:lo + width]

    def publish(q):
        for h in range(2):
            for way in range(2):
                view = piece(h, q, 0, 0)
                g1[h, q, way] = launch(view, view, sg1.at[h, q, way], rg1.at[h, q, way],
                                       along(second_axis[h], step[way]))

    def spread(q, db):
        for h in range(2):
            for way in range(2):
                view = piece(h, q, 0, db)
                g3[h, q, way, db] = launch(view, view, sg3.at[h, q, way, db], rg3.at[h, q, way, db],
                                           along(first_axis[h], step[way]))

    def pass_on(q):
        for way in range(2):
            for h in range(2):
                g1[h, q, way].wait_recv()
                view = piece(h, q, 0, step[1 - way], way)
                g2[h, q, way] = launch(view, view, sg2.at[h, q, way], rg2.at[h, q, way],
                                       along(second_axis[h], step[way]))

    def settle(q):
        for h in range(2):
            for way in range(2):
                g2[h, q, way].wait_recv()

    def forward(q, db):
        for h in range(2):
            for way in range(2):
                g3[h, q, way, db].wait_recv()
                view = piece(h, q, step[1 - way], db, way)
                g4[h, q, way, db] = launch(view, view, sg4.at[h, q, way, db], rg4.at[h, q, way, db],
                                           along(first_axis[h], step[way]))

    fi = gather_ids(0)
    for copy in in_w:
        copy.wait()
    fw = gather_w(0)
    compute(0, 0)
    send_ready(0, 0)
    for k in range(SPLITS[0][1], SPLITS[0][2]):
        hid_in[0, k].wait()
    normalise(0, 1)
    compute(0, 1, following=(0, 2))
    send_ready(0, 1)
    arrive(fi)
    fi = gather_ids(1)
    compute(0, 2, following=(0, 3))
    send_ready(0, 2)
    relay_1(0, 2)
    arrive(fi)
    serve()
    fx = send_rows(0)
    arrive(fw)
    fw = gather_w(1)
    compute(0, 3, following=(1, 0))
    send_ready(0, 3)
    relay_1(0, 1)
    relay_1(0, 3)
    relay_1(0, 0)
    sum_1(0, 2)
    compute(1, 0, following=(1, 1))
    send_ready(1, 0)
    arrive(fx)
    fx = send_rows(1)
    compute(1, 1)
    sum_1(0, 1)
    sum_1(0, 3)
    relay_2(0)
    send_ready(1, 1)
    arrive(fw)
    fw = gather_w(2)
    relay_1(1, 2)
    relay_1(1, 1)
    relay_1(1, 3)
    relay_1(1, 0)
    sum_1(0, 0)
    sum_1(1, 2)
    arrive(fx)
    in_own.wait()
    look()
    arrive(fw)
    finish(0)
    n0 = len(started)
    publish(0)
    spread(0, 0)
    sum_1(1, 1)
    sum_1(1, 3)
    relay_2(1)
    pass_on(0)
    spread(0, 1)
    spread(0, 3)
    sum_1(1, 0)
    settle(0)
    spread(0, 2)
    finish(1)
    n1 = len(started)
    publish(1)
    spread(1, 0)
    drain(n0)
    forward(0, 0)
    pass_on(1)
    spread(1, 1)
    spread(1, 3)
    forward(0, 1)
    forward(0, 3)
    settle(1)
    spread(1, 2)
    forward(0, 2)
    n2 = len(started)
    forward(1, 0)
    drain(n1)
    for db in (1, 3, 2):
        forward(1, db)
    drain(n2)
    arrive(g4.values())
    drain(len(started))


def per_device(
    hidden, token_slab, token_row, slab_owner, ple_table, norm_gains, w_gate, w_up, w_down, ple_gate, ple_proj
):
    members = lax.axis_size("member")
    nz = lax.axis_size("group") // 2
    tok = token_row.shape[0]
    d, n = w_gate.shape[1:]
    slab_rows, pw = ple_table.shape
    half, tq = d // 2, tok // 2
    per = ple_gate.shape[2]
    lanes = d // (2 * nz)
    dma = pltpu.SemaphoreType.DMA
    hbm, vmem = pl.BlockSpec(memory_space=pltpu.HBM), pl.BlockSpec(memory_space=pltpu.VMEM)
    stages = SIDE * SIDE + 2 * nz
    most = max(b - a for split in SPLITS for a, b in zip(split, split[1:]))
    rows_buf = pltpu.VMEM((nz, 2, SIDE, SIDE, 2, pw), BF)
    pairs = [
        (2, 2, 2, 4), (2, 2, 2, 4, 2), (2, 2, 2), (2, 2, 2, 2),
        (2, 2, 2), (2, 2, 2), (2, 2, 2, 4), (2, 2, 2, 4),
        (stages,), (stages,), (stages,),
    ]
    call = pl.pallas_call(
        functools.partial(body, nz, slab_rows),
        out_shape=jax.ShapeDtypeStruct((members, tok, d), BF),
        in_specs=[hbm] * 11,
        out_specs=vmem,
        scratch_shapes=[
            pltpu.VMEM((2, 16, tq, d), BF),
            pltpu.VMEM((tok, d), BF),
            pltpu.VMEM((d, n), BF),
            pltpu.VMEM((d, n), BF),
            pltpu.VMEM((n, d), BF),
            pltpu.VMEM((slab_rows, pw), BF),
            pltpu.VMEM((most * tq, n), BF),
            pltpu.VMEM((2, 2, 16, tq, half), BF),
            pltpu.VMEM((2, 2, 2, 4, tq, half // 2), BF),
            pltpu.VMEM((2, 2, 2, 4, tq, half), BF),
            pltpu.VMEM((2, 2, 2, tq, half // 2), BF),
            pltpu.VMEM((2, 2, 2, tq, half), BF),
            pltpu.VMEM((nz, 2, SIDE, SIDE, 1, tok), F32),
            rows_buf, rows_buf, rows_buf,
            pltpu.VMEM((nz, 2, 2, SIDE, SIDE, per, lanes), BF),
            pltpu.VMEM((3, 1, d), F32),
            pltpu.VMEM((1, tok), jnp.int32),
            pltpu.VMEM((1, tok), jnp.int32),
            pltpu.VMEM((1, slab_owner.shape[0]), jnp.int32),
            pltpu.VMEM((tok, pw), F32),
            dma((48,)),
        ] + [dma(shape) for shape in pairs for _ in range(2)],
        compiler_params=pltpu.CompilerParams(
            collective_id=0, has_side_effects=True, vmem_limit_bytes=40 * 1024 * 1024
        ),
        name="layer",
    )
    operands = (
        hidden.reshape(members, tok, d), w_gate[0], w_up[0], w_down[0], ple_gate[0].T, ple_proj[0], ple_table,
        norm_gains.reshape(3, 1, d), token_slab.reshape(1, tok), token_row.reshape(1, tok),
        slab_owner.reshape(1, -1),
    )
    out = call(*[pltpu.with_memory_space_constraint(v, pltpu.HBM) for v in operands])
    return out.reshape(members * tok, d)


def solution(mesh):
    return jax.shard_map(
        per_device,
        mesh=mesh,
        in_specs=(
            P("group", None),
            P(("group", "member"), None),
            P(("group", "member")),
            P(),
            P(("group", "member"), None),
            P(),
            P(None, None, "member"),
            P(None, None, "member"),
            P(None, "member", None),
            P(None, None, "member"),
            P(None, "member", None),
        ),
        out_specs=P("group", None),
        check_vma=False,
    )
```
